512 devices in a mesh: mode: 32 (over y, x), elem: 16 (over z, core).
Axes of the slice: x: 4, y: 8, z: 8, core: 2. Of those that a mesh axis runs over, the one named last changes fastest.
Arguments:
- rhs_phys: float32 [512, 49152], P(None, ('elem', 'mode')), may hold values from -6 to 6
- radial_basis: float32 [48, 128, 128], P('elem'), may hold values from -0.5 to 0.5
- axial_basis: float32 [48, 7, 7], P('elem'), may hold values from -2 to 2
- radial_eig: float32 [48, 128], P('elem'), may hold values from 0.25 to 8
- axial_eig: float32 [48, 7], P('elem'), may hold values from 0.25 to 8
- face_stiff: float32 [48, 128, 128], P('elem'), may hold values from -0.5 to 0.5
- face_mass: float32 [48, 128, 128], P('elem'), may hold values from -0.5 to 0.5
- axial_coupling: float32 [48, 2, 7], P('elem'), may hold values from -3 to 3
- face_numbering: int32 [48, 2, 128], P('elem'), may hold values from 0 to 127, each once within a row
- band_panels: float32 [2, 48, 128, 128], P(None, 'elem'), may hold values from -1 to 1
- inverse_panels: float32 [256, 48, 128, 128], P('mode', 'elem'), may hold values from -2 to 2
Outputs:
- pressure: float32 [512, 49152], P('mode', 'elem')
The draws below stay inside these ranges and needn't reach their ends.
Inputs may be any that keep to these rules, and one draw needn't show every extreme that they name: Each row of face_numbering is a permutation of 0 to 127.
All inputs are finite; a program needn't handle non-finite values.
Results may differ from the reference program's by a relative error of at most 0.0003.
Values sent between devices are 32-bit elements; how exact they have to be, the bound alone decides.
A program may use at most 64 MiB of HBM per device.

```python
import math
import jax
import jax.numpy as jnp
from jax import lax

RADIAL = 128
INNER = 7
FOURIER_COUNT = 256
PLANES = 512
SLAB_COUNT = 48
NODES = 49152


def panel_noise(key, shape, scales):
    noise = jax.random.truncated_normal(key, -4.0, 4.0, shape, jnp.float32)
    off_diag = 1.0 - jnp.eye(RADIAL, dtype=jnp.float32)
    return noise * off_diag * (0.22 / jnp.sqrt(jnp.float32(RADIAL))) * scales[..., :, None]


def band_parts(key):
    first = jax.random.uniform(jax.random.fold_in(key, 11), (SLAB_COUNT, RADIAL), jnp.float32, 0.5, 1.0)
    second = jax.random.uniform(jax.random.fold_in(key, 12), (SLAB_COUNT, RADIAL), jnp.float32, 0.1, 0.3)
    return (first, second)


def draw_band_panels(key, part):
    first, second = band_parts(key)
    identity_mat = jnp.eye(RADIAL, dtype=jnp.float32)
    lead = identity_mat * first[..., None] + panel_noise(jax.random.fold_in(key, 13), (SLAB_COUNT, RADIAL, RADIAL), first)
    extra = identity_mat * second[..., None] + panel_noise(jax.random.fold_in(key, 14), (SLAB_COUNT, RADIAL, RADIAL), second)
    return jnp.stack([lead, extra])


def draw_inverse_panels(key, part):
    first, second = band_parts(key)
    wavenumber = jnp.arange(FOURIER_COUNT, dtype=jnp.float32) / FOURIER_COUNT
    wavenumber_squared = 4.0 * wavenumber * wavenumber
    diag_band = first[None] + wavenumber_squared[:, None, None] * second[None]
    slow_share = 0.5
    picks = jax.random.uniform(jax.random.fold_in(key, 21), (FOURIER_COUNT, 1, RADIAL), jnp.float32)
    depth = jax.random.uniform(jax.random.fold_in(key, 22), (FOURIER_COUNT, SLAB_COUNT, RADIAL), jnp.float32, 0.5, 1.0)
    slow_rate = jnp.exp(jnp.log(0.2) / SLAB_COUNT * depth)
    fast_rate = jax.random.uniform(jax.random.fold_in(key, 23), (FOURIER_COUNT, SLAB_COUNT, RADIAL), jnp.float32, 0.3, 0.6)
    decay_rates = jnp.where(picks < slow_share, slow_rate, fast_rate)
    interface_batch = jax.random.uniform(jax.random.fold_in(key, 24), (FOURIER_COUNT, SLAB_COUNT, 1), jnp.float32) < 2.0 / SLAB_COUNT
    truncation_factor = jax.random.uniform(jax.random.fold_in(key, 25), (FOURIER_COUNT, SLAB_COUNT, 1), jnp.float32, 0.5, 0.8)
    decay_rates = jnp.where(interface_batch, decay_rates * truncation_factor, decay_rates)
    diag_inverse = decay_rates / diag_band
    identity_mat = jnp.eye(RADIAL, dtype=jnp.float32)
    return identity_mat * diag_inverse[..., None] + panel_noise(jax.random.fold_in(key, 26), (FOURIER_COUNT, SLAB_COUNT, RADIAL, RADIAL), diag_inverse)


def block_levels(own_key, dims, pieces, least, top_value):
    def one(axis_at, blocks):
        heights = jax.random.uniform(jax.random.fold_in(jax.random.fold_in(own_key, 6), axis_at), (blocks,), jnp.float32, least / len(pieces), top_value / len(pieces))
        return jnp.repeat(jnp.exp(heights), dims[axis_at] // blocks).reshape((-1,) + (1,) * (len(dims) - axis_at - 1))

    gain = one(*pieces[0])
    for cut in pieces[1:]:
        gain = gain * one(*cut)
    return gain


def bell_draw(own_key, shape, deviation, most, shards=(), kind=jnp.bfloat16):
    array = jax.random.normal(own_key, shape, jnp.float32) * deviation
    if len(shards) > 0:
        array = block_levels(own_key, shape, shards, -0.22, 0.18) * array
    return jnp.clip(array, min=-most, max=most).astype(kind)


def setup_inputs(seed: int = 0) -> dict:
    key_list = jax.random.split(jax.random.key(seed), 12)
    return {
        "rhs_phys": bell_draw(key_list[0], (PLANES, NODES), 1.0, 6.0, ((1, 512),), jnp.float32),
        "radial_basis": bell_draw(key_list[1], (SLAB_COUNT, RADIAL, RADIAL), RADIAL ** -0.5, 0.5, ((0, 16),), jnp.float32),
        "axial_basis": bell_draw(key_list[2], (SLAB_COUNT, INNER, INNER), INNER ** -0.5, 2.0, ((0, 16),), jnp.float32),
        "radial_eig": jnp.clip(jnp.exp(math.log(8.0) - 3.465736 * jax.random.uniform(key_list[3], (SLAB_COUNT, RADIAL), jnp.float32) ** block_levels(key_list[3], (SLAB_COUNT, RADIAL), ((0, 16),), -0.2, 0.2)), 0.25, 8.0),
        "axial_eig": jnp.clip(jnp.exp(math.log(8.0) - 3.465736 * jax.random.uniform(key_list[4], (SLAB_COUNT, INNER), jnp.float32) ** block_levels(key_list[4], (SLAB_COUNT, INNER), ((0, 16),), -0.2, 0.2)), 0.25, 8.0),
        "face_stiff": bell_draw(key_list[5], (SLAB_COUNT, RADIAL, RADIAL), RADIAL ** -0.5, 0.5, ((0, 16),), jnp.float32),
        "face_mass": bell_draw(key_list[6], (SLAB_COUNT, RADIAL, RADIAL), RADIAL ** -0.5, 0.5, ((0, 16),), jnp.float32),
        "axial_coupling": bell_draw(key_list[7], (SLAB_COUNT, 2, INNER), 0.5, 3.0, ((0, 16),), jnp.float32),
        "face_numbering": jax.vmap(lambda own: jax.random.permutation(own, RADIAL))(jax.random.split(key_list[8], SLAB_COUNT * 2)).reshape((SLAB_COUNT, 2, RADIAL)).astype(jnp.int32),
        "band_panels": draw_band_panels(jax.random.fold_in(key_list[11], 71), 0),
        "inverse_panels": draw_inverse_panels(jax.random.fold_in(key_list[11], 71), 0),
    }


HIGHEST = lax.Precision.HIGHEST

def inverse_interior(values, radial_basis, axial_basis, denominator):
    section_one = jnp.einsum('cjar,jrs->cjas', values, radial_basis, precision=HIGHEST)
    section_one = jnp.einsum('cjas,jab->cjbs', section_one, axial_basis, precision=HIGHEST)
    section_one = section_one / denominator[None]
    section_one = jnp.einsum('cjbs,jrs->cjbr', section_one, radial_basis, precision=HIGHEST)
    return jnp.einsum('cjbr,jab->cjar', section_one, axial_basis, precision=HIGHEST)

def reference(rhs_phys, radial_basis, axial_basis, radial_eig, axial_eig, face_stiff, face_mass, axial_coupling, face_numbering, band_panels, inverse_panels):
    transform = jnp.fft.rfft(rhs_phys, axis=0)[:FOURIER_COUNT] / jnp.sqrt(jnp.float32(PLANES))
    spectrum = jnp.stack([jnp.real(transform), jnp.imag(transform)], axis=1)
    onehot = (face_numbering[..., None] == jnp.arange(RADIAL, dtype=jnp.int32)).astype(jnp.float32)

    def solve_mode(inputs):
        mode_index, modal, panels = inputs
        wavenumber = mode_index.astype(jnp.float32) / FOURIER_COUNT
        wavenumber_squared = 4.0 * wavenumber * wavenumber
        fields = modal.reshape(2, SLAB_COUNT, INNER + 1, RADIAL)
        source_in = fields[:, :, :INNER]
        source_bd = fields[:, :, INNER]
        denominator = axial_eig[:, :, None] + radial_eig[:, None, :] + wavenumber_squared
        solved_values = inverse_interior(source_in, radial_basis, axial_basis, denominator)
        face_sums = jnp.einsum('cjar,jsa->cjsr', solved_values, axial_coupling, precision=HIGHEST)
        pushed = jnp.einsum('cjsr,jrq->cjsq', face_sums, face_stiff, precision=HIGHEST) + wavenumber_squared * jnp.einsum('cjsr,jrq->cjsq', face_sums, face_mass, precision=HIGHEST)
        placed = jnp.einsum('cjsq,jsqp->cjsp', pushed, onehot, precision=HIGHEST)
        from_right = jnp.concatenate([placed[:, 1:, 0], jnp.zeros((2, 1, RADIAL), jnp.float32)], axis=1)
        reduced = source_bd - placed[:, :, 1] - from_right
        coupling = band_panels[0] + wavenumber_squared * band_panels[1]

        def forward_step(carried, parts):
            panel, band, source = parts
            inner_term = source - jnp.einsum('rs,cs->cr', band, carried, precision=HIGHEST)
            value = jnp.einsum('rs,cs->cr', panel, inner_term, precision=HIGHEST)
            return (value, value)
        zero_vec = jnp.zeros((2, RADIAL), jnp.float32)
        unused_one, forward_vals = lax.scan(forward_step, zero_vec, (panels, coupling, jnp.moveaxis(reduced, 1, 0)))
        next_band = jnp.concatenate([coupling[1:], jnp.zeros((1, RADIAL, RADIAL), jnp.float32)], axis=0)

        def backward_step(carried, parts):
            panel, band, value = parts
            solution = value - jnp.einsum('rs,cs->cr', panel, carried, precision=HIGHEST)
            return (jnp.einsum('rs,cr->cs', band, solution, precision=HIGHEST), solution)
        shifted_band = coupling
        unused_two, back_vals = lax.scan(backward_step, zero_vec, (panels, shifted_band, forward_vals), reverse=True)
        interface = jnp.moveaxis(back_vals, 0, 1)
        previous = jnp.concatenate([jnp.zeros((2, 1, RADIAL), jnp.float32), interface[:, :-1]], axis=1)
        face_vals = jnp.stack([previous, interface], axis=2)
        local_face = jnp.einsum('cjsp,jsqp->cjsq', face_vals, onehot, precision=HIGHEST)
        lifted = jnp.einsum('jrq,cjsq->cjsr', face_stiff, local_face, precision=HIGHEST) + wavenumber_squared * jnp.einsum('jrq,cjsq->cjsr', face_mass, local_face, precision=HIGHEST)
        spread = jnp.einsum('cjsr,jsa->cjar', lifted, axial_coupling, precision=HIGHEST)
        interior_values = solved_values - inverse_interior(spread, radial_basis, axial_basis, denominator)
        assembled = jnp.concatenate([interior_values, interface[:, :, None]], axis=2)
        return assembled.reshape(2, NODES)
    solutions = lax.map(solve_mode, (jnp.arange(FOURIER_COUNT, dtype=jnp.int32), spectrum, inverse_panels))
    return solutions.reshape(PLANES, NODES)
```

```python
import functools
import math

import jax
import jax.numpy as jnp
import numpy as np
from jax import lax
from jax.experimental import pallas as pl
from jax.experimental.pallas import tpu as pltpu
from jax.sharding import PartitionSpec as P

F32 = jnp.float32
BF16 = jnp.bfloat16
HIGH = lax.Precision.HIGH


def split(x):
    hi = x.astype(BF16)
    return hi, (x - hi.astype(F32)).astype(BF16)


def bdot(a, b):
    return jnp.dot(a, b, preferred_element_type=F32)


def mul_split(v, hi, lo):
    vh, vl = split(v)
    return bdot(vh, hi) + (bdot(vl, hi) + bdot(vh, lo))


def mul(a, b):
    return mul_split(a, *split(b))


def wave_square(index, mode_total):
    wave = index.astype(F32) / mode_total
    return 4.0 * wave * wave


def store_split(ref, at, x):
    hi, lo = split(x)
    ref[at + (0,)] = hi
    ref[at + (1,)] = lo


def slab_kernel(radial_ref, stiff_ref, mass_ref, number_ref, band_ref, rs_ref, rts_ref, push_ref, lift_ref, es_ref, ets_ref):
    slabs, n = radial_ref.shape[0], radial_ref.shape[1]
    for j in range(slabs):
        basis = radial_ref[j]
        store_split(rs_ref, (j,), basis)
        store_split(rts_ref, (j,), basis.T)
        for part, face in enumerate((stiff_ref, mass_ref)):
            turned = mul(face[j].T, basis)
            th, tl = split(turned)
            for side in range(2):
                numbers = number_ref[2 * j + side : 2 * j + side + 1, :]
                hot = (lax.broadcasted_iota(jnp.int32, (n, n), 0) == numbers).astype(F32).astype(BF16)
                kt = bdot(hot, th) + bdot(hot, tl)
                for ref, x in ((lift_ref, kt), (push_ref, kt.T)):
                    hi, lo = split(x)
                    ref[j, side, 0, part * n : (part + 1) * n, :] = hi
                    ref[j, side, 1, part * n : (part + 1) * n, :] = lo
        if j > 0:
            for part in range(2):
                band = band_ref[part, j]
                for ref, x in ((es_ref, band), (ets_ref, band.T)):
                    hi, lo = split(x)
                    ref[j - 1, 0, part * n : (part + 1) * n, :] = hi
                    ref[j - 1, 1, part * n : (part + 1) * n, :] = lo


def map_kernel(group, mode_dev, mode_total, panel_ref, band_ref, maps_ref, pts_ref, uts_ref, nts_ref):
    step = pl.program_id(0)
    first = lax.axis_index("mode") * mode_dev + step * group
    slabs = panel_ref.shape[1]
    bands = [[band_ref[p, j] for p in range(2)] for j in range(slabs)]
    turned = [[bands[j][p].T for p in range(2)] for j in range(slabs)]
    for i in range(group):
        lam = wave_square(first + i, mode_total)
        e = [bands[j][0] + lam * bands[j][1] for j in range(slabs)]
        et = [split(turned[j][0] + lam * turned[j][1]) for j in range(slabs)]
        es = [split(x) for x in e]
        pt = []
        for j in range(slabs):
            x = split(panel_ref[i, j].T)
            pts_ref[i, j, 0] = x[0]
            pts_ref[i, j, 1] = x[1]
            pt.append(x)

        def times(a, b):
            return bdot(a[0], b[0]) + (bdot(a[1], b[0]) + bdot(a[0], b[1]))

        ahead = []
        now = None
        for j in range(slabs):
            first_factor = et[0] if j == 0 else split(times(now, et[j]))
            full = -times(first_factor, pt[j])
            now = split(full)
            nts_ref[i, j, 0] = now[0]
            nts_ref[i, j, 1] = now[1]
            ahead.append(now)
        maps_ref[i, 0] = full
        back = []
        now = es[0]
        for j in range(slabs):
            if j > 0:
                now = split(times(es[j], now))
            uts_ref[i, j, 0] = now[0]
            uts_ref[i, j, 1] = now[1]
            back.append(now)
            full = -times(pt[j], now)
            now = split(full)
        maps_ref[i, 1] = full
        cross = times(ahead[0], back[0])
        for j in range(1, slabs):
            cross = cross + times(ahead[j], back[j])
        maps_ref[i, 2] = cross


def solve_kernel(
    mode_axis,
    mode_dev,
    mode_total,
    chips,
    axial_ref,
    couple_ref,
    axial_eig_ref,
    spec_ref,
    radial_eig_ref,
    rs_ref,
    rts_ref,
    push_ref,
    lift_ref,
    es_ref,
    ets_ref,
    maps_ref,
    pts_ref,
    uts_ref,
    nts_ref,
    out_ref,
    modal,
    placed_in,
    x_in,
    x_send,
    push_send,
    pair_maps,
    chip_maps,
    own_maps,
    vec_send,
    pair_vecs,
    chip_vecs,
    own_vecs,
    back_send,
    back_vecs,
    fin_send,
    fin,
    sem_pm,
    sem_cm_s,
    sem_cm_r,
    sem_pl,
    sem_pv,
    sem_cv_s,
    sem_cv_r,
    sem_bk_s,
    sem_bk_r,
    sem_fn,
    sem_x,
):
    slabs, n = rs_ref.shape[0], rs_ref.shape[-1]
    rows = 2 * mode_dev
    half = mode_dev // 2
    inner = axial_ref.shape[0] // slabs
    me = lax.axis_index("elem")
    count = 2 * chips
    core = lax.rem(me, 2)
    chip = me // 2
    other = 1 - core
    partner = 2 * chip + other
    across = lax.rem(me + count - 1 + 2 * core, count)

    barrier = pltpu.get_barrier_semaphore()
    for k in range(1, chips):
        pl.semaphore_signal(barrier, 1, device_id={"elem": 2 * lax.rem(chip + k, chips) + core})
    pl.semaphore_signal(barrier, 1, device_id={"elem": partner})
    pl.semaphore_signal(barrier, 1, device_id={"elem": across})

    def remote(src, dst, send, recv, device):
        return pltpu.make_async_remote_copy(
            src, dst, send, recv, device_id={"elem": device}, device_id_type=pl.DeviceIdType.MESH
        )

    row = lax.broadcasted_iota(jnp.int32, (rows, n), 0)
    lam = wave_square(lax.axis_index("mode") * mode_dev + row // 2, mode_total)

    def banded(v, ref):
        return mul_split(jnp.concatenate([v, lam * v], axis=1), ref[0], ref[1])

    def per_mode(v, ref, *at):
        vh, vl = split(v)
        both = jnp.concatenate([vh, vl], axis=0)
        sides = lax.broadcasted_iota(jnp.int32, (2 * rows, n), 0)
        sides = jnp.where(sides < rows, sides, sides - rows) // 2
        zero = jnp.zeros_like(both)
        total = None
        low = None
        for m in range(mode_dev):
            mine = jnp.where(sides == m, both, zero)
            term = bdot(mine, ref[(m,) + at + (0,)])
            term_low = bdot(mine[:rows], ref[(m,) + at + (1,)])
            total = term if total is None else total + term
            low = term_low if low is None else low + term_low
        return total[:rows] + (total[rows:] + low)

    width = spec_ref.shape[2]
    for t in range(slabs * (inner + 1)):
        pieces = []
        at = t * n
        while at < (t + 1) * n:
            source = at // width
            stop = min((t + 1) * n, (source + 1) * width)
            pieces.append(spec_ref[source, :, at - source * width : stop - source * width])
            at = stop
        modal[t] = pieces[0] if len(pieces) == 1 else jnp.concatenate(pieces, axis=1)

    pl.semaphore_wait(barrier, chips + 1)
    share = remote(
        maps_ref.at[pl.ds(half * other, half)], pair_maps.at[core], sem_pm.at[0], sem_pm.at[1], partner
    )
    share.start()

    spectral = []
    inverses = []
    placed = []
    for j in range(slabs):
        base = j * (inner + 1)
        x = jnp.concatenate([modal[base + a] for a in range(inner)], axis=0)
        x = mul_split(x, rs_ref[j, 0], rs_ref[j, 1])
        values = []
        scales = []
        for b in range(inner):
            total = x[:rows] * axial_ref[j * inner, b]
            for a in range(1, inner):
                total = total + x[a * rows : (a + 1) * rows] * axial_ref[j * inner + a, b]
            scale = 1.0 / (axial_eig_ref[j, b] + radial_eig_ref[j : j + 1, :] + lam)
            scales.append(scale)
            values.append(total * scale)
        spectral.append(values)
        inverses.append(scales)
        sums = [None, None]
        for a in range(inner):
            total = values[0] * axial_ref[j * inner + a, 0]
            for b in range(1, inner):
                total = total + values[b] * axial_ref[j * inner + a, b]
            for side in range(2):
                term = total * couple_ref[2 * j + side, a]
                sums[side] = term if sums[side] is None else sums[side] + term
        placed.append([banded(sums[side], push_ref.at[j, side]) for side in range(2)])
        if j == 0:
            push_send[...] = placed[0][0]

            @pl.when(me > 0)
            def _():
                remote(push_send, placed_in, sem_pl.at[0], sem_pl.at[1], me - 1).start()

    pair_maps[core] = maps_ref[pl.ds(half * core, half)]
    share.wait()
    for i in range(half):
        a0, b0, c0 = (pair_maps[0, i, k] for k in range(3))
        a1, b1, c1 = (pair_maps[1, i, k] for k in range(3))
        a0s, b0s = split(a0), split(b0)
        chip_maps[i, 0] = mul(a0, a1)
        chip_maps[i, 1] = mul_split(b1, *b0s)
        chip_maps[i, 2] = c0 + mul_split(mul(a0, c1), *b0s)
        owner = half * core + i

        @pl.when(owner != chip)
        def _():
            remote(
                chip_maps.at[i], own_maps.at[chip], sem_cm_s.at[i], sem_cm_r.at[chip], 2 * owner + core
            ).start()

        @pl.when(owner == chip)
        def _():
            own_maps[chip] = chip_maps[i]

    loads = [modal[j * (inner + 1) + inner] - placed[j][1] for j in range(slabs)]
    for j in range(slabs - 1):
        loads[j] = loads[j] - placed[j + 1][0]
    local = [per_mode(loads[0], pts_ref, 0)]
    for j in range(1, slabs):
        load = loads[j] - banded(local[j - 1], ets_ref.at[j - 1])
        if j == slabs - 1:

            @pl.when(me == count - 1)
            def _():
                placed_in[...] = jnp.zeros_like(placed_in)

            @pl.when(me < count - 1)
            def _():
                remote(push_send, placed_in, sem_pl.at[0], sem_pl.at[1], me).wait_recv()

            load = load - placed_in[...]
        local.append(per_mode(load, pts_ref, j))
    offset = per_mode(local[0], uts_ref, 0)
    for j in range(1, slabs):
        offset = offset + per_mode(local[j], uts_ref, j)
    vec_send[...] = jnp.zeros_like(vec_send)
    for m in range(mode_dev):
        vec_send[m, 0:2, :] = local[-1][2 * m : 2 * m + 2]
        vec_send[m, 2:4, :] = offset[2 * m : 2 * m + 2]
    swap = remote(
        vec_send.at[pl.ds(half * other, half)], pair_vecs.at[core], sem_pv.at[0], sem_pv.at[1], partner
    )
    swap.start()
    pair_vecs[core] = vec_send[pl.ds(half * core, half)]
    swap.wait()
    low = lax.broadcasted_iota(jnp.int32, (8, n), 0) < 2
    for i in range(half):
        t0, t1 = pair_vecs[0, i], pair_vecs[1, i]
        b0 = pair_maps[0, i, 1]
        a1, c1 = pair_maps[1, i, 0], pair_maps[1, i, 2]
        inside = t1 + pltpu.roll(mul(t0, c1), 2, 0)
        chip_vecs[i] = jnp.where(low, mul(t0, a1) + t1, t0 + mul(inside, b0))
        owner = half * core + i

        @pl.when(owner != chip)
        def _():
            remote(
                chip_vecs.at[i], own_vecs.at[chip], sem_cv_s.at[i], sem_cv_r.at[chip], 2 * owner + core
            ).start()

        @pl.when(owner == chip)
        def _():
            own_vecs[chip] = chip_vecs[i]

    mine = chip - half * core

    @pl.when(chip // half == core)
    def _():
        for z in range(chips):

            @pl.when(z != chip)
            def _():
                remote(chip_maps.at[0], own_maps.at[z], sem_cm_s.at[0], sem_cm_r.at[z], me).wait_recv()
                remote(chip_vecs.at[0], own_vecs.at[z], sem_cv_s.at[0], sem_cv_r.at[z], me).wait_recv()

        state = jnp.zeros((8, n), F32)
        before = []
        terms = []
        for z in range(chips):
            before.append(state)
            if z > 0:
                terms.append(own_vecs[z] + pltpu.roll(mul(state, own_maps[z, 2]), 2, 0))
                state = mul(state, own_maps[z, 0]) + own_vecs[z]
            else:
                terms.append(own_vecs[z])
                state = own_vecs[z]
        state = jnp.zeros((8, n), F32)
        for z in reversed(range(chips)):
            back_send[z] = jnp.where(low, before[z], state)

            @pl.when(z != chip)
            def _():
                remote(back_send.at[z], back_vecs.at[mine], sem_bk_s.at[z], sem_bk_r.at[mine], 2 * z + core).start()

            @pl.when(z == chip)
            def _():
                back_vecs[mine] = back_send[z]

            if z > 0:
                state = terms[z] if z == chips - 1 else mul(state, own_maps[z, 1]) + terms[z]

    for i in range(half):

        @pl.when(half * core + i != chip)
        def _():
            remote(back_send.at[0], back_vecs.at[i], sem_bk_s.at[0], sem_bk_r.at[i], me).wait_recv()

        t0, t1 = pair_vecs[0, i], pair_vecs[1, i]
        a0 = pair_maps[0, i, 0]
        b1, c1 = pair_maps[1, i, 1], pair_maps[1, i, 2]
        ends = back_vecs[i]
        middle = mul(ends, a0) + t0
        turned = mul(ends, b1) + t1 + pltpu.roll(mul(middle, c1), 2, 0)
        for_zero = jnp.where(low, ends, turned)
        for_one = jnp.where(low, middle, ends)
        fin[half * core + i] = jnp.where(core == 0, for_zero, for_one)
        fin_send[i] = jnp.where(core == 0, for_one, for_zero)
    give = remote(fin_send, fin.at[pl.ds(half * core, half)], sem_fn.at[0], sem_fn.at[1], partner)
    give.start()
    give.wait_send()
    remote(fin_send, fin.at[pl.ds(half * other, half)], sem_fn.at[0], sem_fn.at[1], partner).wait_recv()

    start = jnp.concatenate([fin[m, 0:2, :] for m in range(mode_dev)], axis=0)
    end = jnp.concatenate([fin[m, 2:4, :] for m in range(mode_dev)], axis=0)
    values = [None] * slabs
    for j in reversed(range(slabs)):
        full = local[j] + per_mode(start, nts_ref, j)
        values[j] = full - per_mode(end, pts_ref, j)
        if j == slabs - 1:
            x_send[...] = values[j]

            @pl.when(me < count - 1)
            def _():
                remote(x_send, x_in, sem_x.at[0], sem_x.at[1], me + 1).start()

        if j > 0:
            end = banded(values[j], es_ref.at[j - 1])

    for j in reversed(range(slabs)):
        if j == 0:

            @pl.when(me == 0)
            def _():
                x_in[...] = jnp.zeros_like(x_in)

            @pl.when(me > 0)
            def _():
                remote(x_send, x_in, sem_x.at[0], sem_x.at[1], me).wait_recv()

            faces = [x_in[...], values[0]]
        else:
            faces = [values[j - 1], values[j]]
        lifted = [banded(faces[side], lift_ref.at[j, side]) for side in range(2)]
        spread = [
            lifted[0] * couple_ref[2 * j, a] + lifted[1] * couple_ref[2 * j + 1, a] for a in range(inner)
        ]
        left = []
        for b in range(inner):
            total = spread[0] * axial_ref[j * inner, b]
            for a in range(1, inner):
                total = total + spread[a] * axial_ref[j * inner + a, b]
            left.append(spectral[j][b] - total * inverses[j][b])
        turned = []
        for a in range(inner):
            total = left[0] * axial_ref[j * inner + a, 0]
            for b in range(1, inner):
                total = total + left[b] * axial_ref[j * inner + a, b]
            turned.append(total)
        result = mul_split(jnp.concatenate(turned, axis=0), rts_ref[j, 0], rts_ref[j, 1])
        base = j * (inner + 1) * n
        for a in range(inner):
            out_ref[:, base + a * n : base + (a + 1) * n] = result[a * rows : (a + 1) * rows]
        out_ref[:, base + inner * n : base + (inner + 1) * n] = values[j]

    @pl.when(me > 0)
    def _():
        remote(push_send, placed_in, sem_pl.at[0], sem_pl.at[1], me - 1).wait_send()

    @pl.when(me < count - 1)
    def _():
        remote(x_send, x_in, sem_x.at[0], sem_x.at[1], me + 1).wait_send()

    for i in range(half):

        @pl.when(half * core + i != chip)
        def _():
            owner = 2 * (half * core + i) + core
            remote(chip_maps.at[i], own_maps.at[chip], sem_cm_s.at[i], sem_cm_r.at[chip], owner).wait_send()
            remote(chip_vecs.at[i], own_vecs.at[chip], sem_cv_s.at[i], sem_cv_r.at[chip], owner).wait_send()

    @pl.when(chip // half == core)
    def _():
        for z in range(chips):

            @pl.when(z != chip)
            def _():
                remote(back_send.at[z], back_vecs.at[mine], sem_bk_s.at[z], sem_bk_r.at[mine], 2 * z + core).wait_send()


def fourier_table(planes):
    row = np.arange(planes)[:, None]
    angles = (row // 2 * np.arange(planes)[None, :] % planes) * (2.0 * math.pi / planes)
    return (np.where(row % 2 == 0, np.cos(angles), -np.sin(angles)) / math.sqrt(planes)).astype(np.float32)


VMEM = pl.BlockSpec(memory_space=pltpu.VMEM)
SMEM = pl.BlockSpec(memory_space=pltpu.SMEM)


def body(
    rhs_phys,
    radial_basis,
    axial_basis,
    radial_eig,
    axial_eig,
    face_stiff,
    face_mass,
    axial_coupling,
    face_numbering,
    band_panels,
    inverse_panels,
):
    planes = rhs_phys.shape[0]
    mode_dev, slabs, n = inverse_panels.shape[:3]
    inner = axial_basis.shape[1]
    mode_axis = lax.axis_size("mode")
    chips = lax.axis_size("elem") // 2
    mode_total = mode_dev * mode_axis
    rows = 2 * mode_dev
    half = mode_dev // 2
    S = jax.ShapeDtypeStruct

    spectrum = jnp.dot(jnp.asarray(fourier_table(planes)), rhs_phys, precision=HIGH, preferred_element_type=F32)
    spectrum = lax.all_to_all(spectrum.reshape(mode_axis, rows, -1), "mode", split_axis=0, concat_axis=0)

    rs, rts, push, lift, es, ets = pl.pallas_call(
        slab_kernel,
        out_shape=[
            S((slabs, 2, n, n), BF16),
            S((slabs, 2, n, n), BF16),
            S((slabs, 2, 2, 2 * n, n), BF16),
            S((slabs, 2, 2, 2 * n, n), BF16),
            S((slabs - 1, 2, 2 * n, n), BF16),
            S((slabs - 1, 2, 2 * n, n), BF16),
        ],
        in_specs=[VMEM] * 5,
        out_specs=[VMEM] * 6,
        compiler_params=pltpu.CompilerParams(vmem_limit_bytes=32 << 20),
        name="slab_maps",
    )(radial_basis, face_stiff, face_mass, face_numbering.reshape(2 * slabs, n), band_panels)

    group = min(GROUP, mode_dev)
    maps, pts, uts, nts = pl.pallas_call(
        functools.partial(map_kernel, group, mode_dev, mode_total),
        grid=(mode_dev // group,),
        out_shape=[
            S((mode_dev, 3, n, n), F32),
            S((mode_dev, slabs, 2, n, n), BF16),
            S((mode_dev, slabs, 2, n, n), BF16),
            S((mode_dev, slabs, 2, n, n), BF16),
        ],
        in_specs=[
            pl.BlockSpec((group, slabs, n, n), lambda i: (i, 0, 0, 0)),
            pl.BlockSpec((2, slabs, n, n), lambda i: (0, 0, 0, 0)),
        ],
        out_specs=[
            pl.BlockSpec((group, 3, n, n), lambda i: (i, 0, 0, 0)),
            pl.BlockSpec((group, slabs, 2, n, n), lambda i: (i, 0, 0, 0, 0)),
            pl.BlockSpec((group, slabs, 2, n, n), lambda i: (i, 0, 0, 0, 0)),
            pl.BlockSpec((group, slabs, 2, n, n), lambda i: (i, 0, 0, 0, 0)),
        ],
        compiler_params=pltpu.CompilerParams(vmem_limit_bytes=32 << 20),
        name="mode_maps",
    )(inverse_panels, band_panels)

    V = pltpu.VMEM
    D = pltpu.SemaphoreType.DMA
    return pl.pallas_call(
        functools.partial(solve_kernel, mode_axis, mode_dev, mode_total, chips),
        out_shape=S((rows, slabs * (inner + 1) * n), F32),
        in_specs=[SMEM] * 3 + [VMEM] * 12,
        out_specs=VMEM,
        scratch_shapes=[
            V((slabs * (inner + 1), rows, n), F32),
            V((rows, n), F32),
            V((rows, n), F32),
            V((rows, n), F32),
            V((rows, n), F32),
            V((2, half, 3, n, n), F32),
            V((half, 3, n, n), F32),
            V((chips, 3, n, n), F32),
            V((mode_dev, 8, n), F32),
            V((2, half, 8, n), F32),
            V((half, 8, n), F32),
            V((chips, 8, n), F32),
            V((chips, 8, n), F32),
            V((half, 8, n), F32),
            V((half, 8, n), F32),
            V((mode_dev, 8, n), F32),
            D((2,)),
            D((half,)),
            D((chips,)),
            D((2,)),
            D((2,)),
            D((half,)),
            D((chips,)),
            D((chips,)),
            D((half,)),
            D((2,)),
            D((2,)),
        ],
        compiler_params=pltpu.CompilerParams(
            collective_id=0, has_side_effects=True, vmem_limit_bytes=48 << 20
        ),
        name="slab_solve",
    )(
        axial_basis.reshape(slabs * inner, inner),
        axial_coupling.reshape(2 * slabs, inner),
        axial_eig,
        spectrum,
        radial_eig,
        rs,
        rts,
        push,
        lift,
        es,
        ets,
        maps,
        pts,
        uts,
        nts,
    )


GROUP = 4


def solution(mesh):
    placed = (
        P(None, ("elem", "mode")),
        P("elem", None, None),
        P("elem", None, None),
        P("elem", None),
        P("elem", None),
        P("elem", None, None),
        P("elem", None, None),
        P("elem", None, None),
        P("elem", None, None),
        P(None, "elem", None, None),
        P("mode", "elem", None, None),
    )
    return jax.shard_map(
        body, mesh=mesh, in_specs=placed, out_specs=P("mode", "elem"), check_vma=False
    )
```

```python
import functools
import math
from types import SimpleNamespace

import jax
import jax.numpy as jnp
import ml_dtypes
import numpy as np
from jax import lax
from jax.experimental import pallas as pl
from jax.experimental.pallas import tpu as pltpu
from jax.sharding import PartitionSpec as P

F32 = jnp.float32
BF16 = jnp.bfloat16
HIGH = lax.Precision.HIGH


def split(x):
    hi = x.astype(BF16)
    return hi, (x - hi.astype(F32)).astype(BF16)


def bdot(a, b):
    return jnp.dot(a, b, preferred_element_type=F32)


def mul_split(v, hi, lo):
    vh, vl = split(v)
    return bdot(vh, hi) + (bdot(vl, hi) + bdot(vh, lo))


def mul(a, b):
    return mul_split(a, *split(b))


def wave_square(index, mode_total):
    wave = index.astype(F32) / mode_total
    return 4.0 * wave * wave


def store_split(ref, at, x):
    hi, lo = split(x)
    ref[at + (0,)] = hi
    ref[at + (1,)] = lo


def slab_matrices(s, number_ref):
    slabs, n = s.radial.shape[0], s.radial.shape[1]
    turned = []
    for j in range(slabs):
        basis = s.radial[j]
        store_split(s.rs, (j,), basis)
        store_split(s.rts, (j,), basis.T)
        for face in (s.stiff, s.mass):
            turned.append(split(mul(face[j].T, basis)))
    for j in range(slabs):
        for side in range(2):
            numbers = number_ref[2 * j + side : 2 * j + side + 1, :]
            hot = (lax.broadcasted_iota(jnp.int32, (n, n), 0) == numbers).astype(F32).astype(BF16)
            for part in range(2):
                th, tl = turned[2 * j + part]
                kt = bdot(hot, th) + bdot(hot, tl)
                for ref, x in ((s.lift, kt), (s.push, kt.T)):
                    hi, lo = split(x)
                    ref[j, side, 0, part * n : (part + 1) * n, :] = hi
                    ref[j, side, 1, part * n : (part + 1) * n, :] = lo
    for j in range(1, slabs):
        for part in range(2):
            band = s.band[part, j]
            for ref, x in ((s.es, band), (s.ets, band.T)):
                hi, lo = split(x)
                ref[j - 1, 0, part * n : (part + 1) * n, :] = hi
                ref[j - 1, 1, part * n : (part + 1) * n, :] = lo


def times(a, b):
    return bdot(a[0], b[0]) + (bdot(a[1], b[0]) + bdot(a[0], b[1]))


def mode_maps(s, modes, first, mode_total):
    slabs = s.panel.shape[1]
    count = len(modes)
    turned = [[s.band[p, j].T for p in range(2)] for j in range(slabs)]
    lams = [wave_square(first + m, mode_total) for m in modes]
    es = [[split(s.band[0, j] + lam * s.band[1, j]) for j in range(slabs)] for lam in lams]
    ets = [[split(turned[j][0] + lam * turned[j][1]) for j in range(slabs)] for lam in lams]
    pts = [[split(s.panel[m, j].T) for j in range(slabs)] for m in modes]
    for i, m in enumerate(modes):
        for j in range(slabs):
            s.pts[m, j, 0] = pts[i][j][0]
            s.pts[m, j, 1] = pts[i][j][1]
    ahead = [ets[i][0] for i in range(count)]
    back = [es[i][0] for i in range(count)]
    cross = [None] * count
    nears = [[] for _ in modes]
    for j in range(slabs):
        if j > 0:
            for i in range(count):
                ahead[i] = split(times(ahead[i], ets[i][j]))
                back[i] = split(times(es[i][j], back[i]))
        for i, m in enumerate(modes):
            s.uts[m, j, 0] = back[i][0]
            s.uts[m, j, 1] = back[i][1]
            full = -times(ahead[i], pts[i][j])
            ahead[i] = split(full)
            s.nts[m, j, 0] = ahead[i][0]
            s.nts[m, j, 1] = ahead[i][1]
            nears[i].append((ahead[i], back[i]))
            backed = -times(pts[i][j], back[i])
            back[i] = split(backed)
            if j == slabs - 1:
                s.maps[m, 0] = full
                s.maps[m, 1] = backed
    for j in range(slabs):
        for i in range(count):
            term = times(*nears[i][j])
            cross[i] = term if cross[i] is None else cross[i] + term
    for i, m in enumerate(modes):
        s.maps[m, 2] = cross[i]


def solve_kernel(
    names,
    mode_axis,
    mode_dev,
    mode_total,
    chips,
    axial_ref,
    couple_ref,
    axial_eig_ref,
    radial_eig_ref,
    number_ref,
    *refs,
):
    s = SimpleNamespace(**dict(zip(names, refs)))
    out_ref = s.out
    slabs, n = s.rs.shape[0], s.rs.shape[-1]
    rows = 2 * mode_dev
    half = mode_dev // 2
    inner = axial_ref.shape[0] // slabs
    me = lax.axis_index("elem")
    count = 2 * chips
    core = lax.rem(me, 2)
    chip = me // 2
    other = 1 - core
    partner = 2 * chip + other
    across = lax.rem(me + count - 1 + 2 * core, count)

    fetch = []
    for at, name in enumerate(LOADED):
        copy = pltpu.make_async_copy(getattr(s, name + "_hbm"), getattr(s, name), s.sem_in.at[at])
        copy.start()
        fetch.append(copy)

    barrier = pltpu.get_barrier_semaphore()
    line = lax.axis_index("mode")
    for k in range(1, mode_axis):
        pl.semaphore_signal(barrier, 1, device_id={"mode": lax.rem(line + k, mode_axis)})
    for k in range(1, chips):
        pl.semaphore_signal(barrier, 1, device_id={"elem": 2 * lax.rem(chip + k, chips) + core})
    pl.semaphore_signal(barrier, 1, device_id={"elem": partner})
    pl.semaphore_signal(barrier, 1, device_id={"elem": across})

    def remote(src, dst, send, recv, device):
        return pltpu.make_async_remote_copy(
            src, dst, send, recv, device_id={"elem": device}, device_id_type=pl.DeviceIdType.MESH
        )

    row = lax.broadcasted_iota(jnp.int32, (rows, n), 0)
    lam = wave_square(lax.axis_index("mode") * mode_dev + row // 2, mode_total)

    def banded(v, ref):
        return mul_split(jnp.concatenate([v, lam * v], axis=1), ref[0], ref[1])

    def per_mode(v, ref, *at):
        vh, vl = split(v)
        both = jnp.concatenate([vh, vl], axis=0)
        sides = lax.broadcasted_iota(jnp.int32, (2 * rows, n), 0)
        sides = jnp.where(sides < rows, sides, sides - rows) // 2
        zero = jnp.zeros_like(both)
        total = None
        low = None
        for m in range(mode_dev):
            mine = jnp.where(sides == m, both, zero)
            term = bdot(mine, ref[(m,) + at + (0,)])
            term_low = bdot(mine[:rows], ref[(m,) + at + (1,)])
            total = term if total is None else total + term
            low = term_low if low is None else low + term_low
        return total[:rows] + (total[rows:] + low)

    for copy in fetch[:2]:
        copy.wait()
    rhs = split(s.rhs[...])
    spectrum = bdot(s.table[0], rhs[0]) + (bdot(s.table[1], rhs[0]) + bdot(s.table[0], rhs[1]))
    s.spec_out[...] = spectrum.reshape(s.spec_out.shape)
    for copy in fetch[2:4]:
        copy.wait()
    first = line * mode_dev
    quarter = max(half // 2, 1)
    parts = [range(at, min(at + quarter, half)) for at in range(0, half, quarter)]
    pl.semaphore_wait(barrier, mode_axis + chips)

    def spread_out(k, carry):
        to = lax.rem(line + k, mode_axis)
        pltpu.make_async_remote_copy(
            s.spec_out.at[to],
            s.spec_in.at[line],
            s.sem_sp.at[0],
            s.sem_sp.at[1],
            device_id={"mode": to},
            device_id_type=pl.DeviceIdType.MESH,
        ).start()
        return carry

    lax.fori_loop(1, mode_axis, spread_out, 0)
    s.spec_in[line] = s.spec_out[line]

    shares = []
    for at, part in enumerate(parts):
        modes = [half * other + i for i in part] + [half * core + i for i in part]
        mode_maps(s, modes, first, mode_total)
        share = remote(
            s.maps.at[pl.ds(half * other + part[0], len(part))],
            s.pair_maps.at[core, pl.ds(part[0], len(part))],
            s.sem_pm_s.at[at],
            s.sem_pm_r.at[at],
            partner,
        )
        share.start()
        shares.append(share)

    s.pair_maps[core] = s.maps[pl.ds(half * core, half)]

    def send_map(i, start):
        owner = half * core + i
        away = jnp.logical_and(owner != chip, chip > 0)
        to = 2 * owner + core
        ends = remote(
            s.chip_maps.at[i, pl.ds(0, 2)],
            s.own_maps.at[chip, pl.ds(0, 2)],
            s.sem_cm_s.at[i, 0],
            s.sem_cm_r.at[chip, 0],
            to,
        )
        cross = remote(
            s.chip_maps.at[i, 2], s.own_maps.at[chip, 2], s.sem_cm_s.at[i, 1], s.sem_cm_r.at[chip, 1], to
        )

        @pl.when(jnp.logical_and(away, chip < chips - 1))
        def _():
            ends.start() if start else ends.wait_send()

        @pl.when(away)
        def _():
            cross.start() if start else cross.wait_send()

    for part, share in zip(parts, shares):
        share.wait()
        pair = [[[split(s.pair_maps[c, i, k]) for k in range(3)] for c in range(2)] for i in part]
        ahead = [times(one[0][0], one[1][0]) for one in pair]
        back = [times(one[1][1], one[0][1]) for one in pair]
        cross = [split(times(one[0][0], one[1][2])) for one in pair]
        cross = [times(x, one[0][1]) for x, one in zip(cross, pair)]
        for at, i in enumerate(part):
            s.chip_maps[i, 0] = ahead[at]
            s.chip_maps[i, 1] = back[at]
            s.chip_maps[i, 2] = s.pair_maps[0, i, 2] + cross[at]
        for i in part:
            send_map(i, True)

            @pl.when(half * core + i == chip)
            def _():
                s.own_maps[chip] = s.chip_maps[i]

    for copy in fetch[4:]:
        copy.wait()
    slab_matrices(s, number_ref)

    others = s.spec_in.at[pl.ds(0, mode_axis - 1)]
    pltpu.make_async_remote_copy(
        others, others, s.sem_sp.at[0], s.sem_sp.at[1], device_id={"mode": line}, device_id_type=pl.DeviceIdType.MESH
    ).wait()
    width = s.spec_in.shape[2]
    modal = []
    for t in range(slabs * (inner + 1)):
        pieces = []
        at = t * n
        while at < (t + 1) * n:
            source = at // width
            stop = min((t + 1) * n, (source + 1) * width)
            pieces.append(s.spec_in[source, :, at - source * width : stop - source * width])
            at = stop
        modal.append(pieces[0] if len(pieces) == 1 else jnp.concatenate(pieces, axis=1))

    spectral = []
    inverses = []
    sums = []
    fields = []
    for j in range(slabs):
        base = j * (inner + 1)
        x = jnp.concatenate([modal[base + a] for a in range(inner)], axis=0)
        fields.append(mul_split(x, s.rs[j, 0], s.rs[j, 1]))
    for j in range(slabs):
        x = fields[j]
        values = []
        scales = []
        for b in range(inner):
            total = x[:rows] * axial_ref[j * inner, b]
            for a in range(1, inner):
                total = total + x[a * rows : (a + 1) * rows] * axial_ref[j * inner + a, b]
            scale = 1.0 / (axial_eig_ref[j, b] + radial_eig_ref[j : j + 1, :] + lam)
            scales.append(scale)
            values.append(total * scale)
        spectral.append(values)
        inverses.append(scales)
        faces = [None, None]
        for a in range(inner):
            total = values[0] * axial_ref[j * inner + a, 0]
            for b in range(1, inner):
                total = total + values[b] * axial_ref[j * inner + a, b]
            for side in range(2):
                term = total * couple_ref[2 * j + side, a]
                faces[side] = term if faces[side] is None else faces[side] + term
        sums.append(faces)
        if j == 0:
            s.push_send[...] = banded(faces[0], s.push.at[0, 0])

            @pl.when(me > 0)
            def _():
                remote(s.push_send, s.placed_in, s.sem_pl.at[0], s.sem_pl.at[1], me - 1).start()

    placed = [
        [None if j + side == 0 else banded(sums[j][side], s.push.at[j, side]) for side in range(2)]
        for j in range(slabs)
    ]

    loads = [modal[j * (inner + 1) + inner] - placed[j][1] for j in range(slabs)]
    for j in range(slabs - 1):
        loads[j] = loads[j] - placed[j + 1][0]
    local = [per_mode(loads[0], s.pts, 0)]
    for j in range(1, slabs):
        load = loads[j] - banded(local[j - 1], s.ets.at[j - 1])
        if j == slabs - 1:

            @pl.when(me == count - 1)
            def _():
                s.placed_in[...] = jnp.zeros_like(s.placed_in)

            @pl.when(me < count - 1)
            def _():
                remote(s.push_send, s.placed_in, s.sem_pl.at[0], s.sem_pl.at[1], me).wait_recv()

            load = load - s.placed_in[...]
        local.append(per_mode(load, s.pts, j))
    offset = per_mode(local[0], s.uts, 0)
    for j in range(1, slabs):
        offset = offset + per_mode(local[j], s.uts, j)
    s.vec_send[...] = jnp.zeros_like(s.vec_send)
    for m in range(mode_dev):
        s.vec_send[m, 0:2, :] = local[-1][2 * m : 2 * m + 2]
        s.vec_send[m, 2:4, :] = offset[2 * m : 2 * m + 2]
    swap = remote(
        s.vec_send.at[pl.ds(half * other, half)], s.pair_vecs.at[core], s.sem_pv.at[0], s.sem_pv.at[1], partner
    )
    swap.start()
    s.pair_vecs[core] = s.vec_send[pl.ds(half * core, half)]
    swap.wait()
    low = lax.broadcasted_iota(jnp.int32, (8, n), 0) < 2
    for i in range(half):
        t0, t1 = s.pair_vecs[0, i], s.pair_vecs[1, i]
        b0 = s.pair_maps[0, i, 1]
        a1, c1 = s.pair_maps[1, i, 0], s.pair_maps[1, i, 2]
        inside = t1 + pltpu.roll(mul(t0, c1), 2, 0)
        s.chip_vecs[i] = jnp.where(low, mul(t0, a1) + t1, t0 + mul(inside, b0))
        owner = half * core + i

        @pl.when(owner != chip)
        def _():
            remote(
                s.chip_vecs.at[i], s.own_vecs.at[chip], s.sem_cv_s.at[i], s.sem_cv_r.at[chip], 2 * owner + core
            ).start()

        @pl.when(owner == chip)
        def _():
            s.own_vecs[chip] = s.chip_vecs[i]

    mine = chip - half * core

    @pl.when(chip // half == core)
    def _():
        for z in range(chips):

            @pl.when(z != chip)
            def _():
                remote(s.chip_vecs.at[0], s.own_vecs.at[z], s.sem_cv_s.at[0], s.sem_cv_r.at[z], me).wait_recv()
                two = pl.ds(0, 2)
                if 0 < z < chips - 1:
                    remote(
                        s.chip_maps.at[0, two], s.own_maps.at[z, two], s.sem_cm_s.at[0, 0], s.sem_cm_r.at[z, 0], me
                    ).wait_recv()
                if z > 0:
                    remote(
                        s.chip_maps.at[0, 2], s.own_maps.at[z, 2], s.sem_cm_s.at[0, 1], s.sem_cm_r.at[z, 1], me
                    ).wait_recv()

        state = jnp.zeros((8, n), F32)
        before = []
        terms = []
        for z in range(chips):
            before.append(state)
            if z > 0:
                terms.append(s.own_vecs[z] + pltpu.roll(mul(state, s.own_maps[z, 2]), 2, 0))
                if z < chips - 1:
                    state = mul(state, s.own_maps[z, 0]) + s.own_vecs[z]
            else:
                terms.append(s.own_vecs[z])
                state = s.own_vecs[z]
        state = jnp.zeros((8, n), F32)
        for z in reversed(range(chips)):
            s.back_send[z] = jnp.where(low, before[z], state)

            @pl.when(z != chip)
            def _():
                remote(s.back_send.at[z], s.back_vecs.at[mine], s.sem_bk_s.at[z], s.sem_bk_r.at[mine], 2 * z + core).start()

            @pl.when(z == chip)
            def _():
                s.back_vecs[mine] = s.back_send[z]

            if z > 0:
                state = terms[z] if z == chips - 1 else mul(state, s.own_maps[z, 1]) + terms[z]

    for i in range(half):

        @pl.when(half * core + i != chip)
        def _():
            remote(s.back_send.at[0], s.back_vecs.at[i], s.sem_bk_s.at[0], s.sem_bk_r.at[i], me).wait_recv()

        t0, t1 = s.pair_vecs[0, i], s.pair_vecs[1, i]
        a0 = s.pair_maps[0, i, 0]
        b1, c1 = s.pair_maps[1, i, 1], s.pair_maps[1, i, 2]
        ends = s.back_vecs[i]
        middle = mul(ends, a0) + t0
        turned = mul(ends, b1) + t1 + pltpu.roll(mul(middle, c1), 2, 0)
        for_zero = jnp.where(low, ends, turned)
        for_one = jnp.where(low, middle, ends)
        s.fin[half * core + i] = jnp.where(core == 0, for_zero, for_one)
        s.fin_send[i] = jnp.where(core == 0, for_one, for_zero)
    give = remote(s.fin_send, s.fin.at[pl.ds(half * core, half)], s.sem_fn.at[0], s.sem_fn.at[1], partner)
    give.start()
    give.wait_send()
    remote(s.fin_send, s.fin.at[pl.ds(half * other, half)], s.sem_fn.at[0], s.sem_fn.at[1], partner).wait_recv()

    start = jnp.concatenate([s.fin[m, 0:2, :] for m in range(mode_dev)], axis=0)
    end = jnp.concatenate([s.fin[m, 2:4, :] for m in range(mode_dev)], axis=0)
    values = [None] * slabs
    for j in reversed(range(slabs)):
        full = local[j] + per_mode(start, s.nts, j)
        values[j] = full - per_mode(end, s.pts, j)
        if j == slabs - 1:
            s.x_send[...] = values[j]

            @pl.when(me < count - 1)
            def _():
                remote(s.x_send, s.x_in, s.sem_x.at[0], s.sem_x.at[1], me + 1).start()

        if j > 0:
            end = banded(values[j], s.es.at[j - 1])

    for j in reversed(range(slabs)):
        if j == 0:

            @pl.when(me == 0)
            def _():
                s.x_in[...] = jnp.zeros_like(s.x_in)

            @pl.when(me > 0)
            def _():
                remote(s.x_send, s.x_in, s.sem_x.at[0], s.sem_x.at[1], me).wait_recv()

            faces = [s.x_in[...], values[0]]
        else:
            faces = [values[j - 1], values[j]]
        lifted = [banded(faces[side], s.lift.at[j, side]) for side in range(2)]
        spread = [
            lifted[0] * couple_ref[2 * j, a] + lifted[1] * couple_ref[2 * j + 1, a] for a in range(inner)
        ]
        left = []
        for b in range(inner):
            total = spread[0] * axial_ref[j * inner, b]
            for a in range(1, inner):
                total = total + spread[a] * axial_ref[j * inner + a, b]
            left.append(spectral[j][b] - total * inverses[j][b])
        turned = []
        for a in range(inner):
            total = left[0] * axial_ref[j * inner + a, 0]
            for b in range(1, inner):
                total = total + left[b] * axial_ref[j * inner + a, b]
            turned.append(total)
        result = mul_split(jnp.concatenate(turned, axis=0), s.rts[j, 0], s.rts[j, 1])
        base = j * (inner + 1) * n
        for a in range(inner):
            out_ref[:, base + a * n : base + (a + 1) * n] = result[a * rows : (a + 1) * rows]
        out_ref[:, base + inner * n : base + (inner + 1) * n] = values[j]

    @pl.when(me > 0)
    def _():
        remote(s.push_send, s.placed_in, s.sem_pl.at[0], s.sem_pl.at[1], me - 1).wait_send()

    @pl.when(me < count - 1)
    def _():
        remote(s.x_send, s.x_in, s.sem_x.at[0], s.sem_x.at[1], me + 1).wait_send()

    for i in range(half):
        send_map(i, False)

        @pl.when(half * core + i != chip)
        def _():
            owner = 2 * (half * core + i) + core
            remote(s.chip_vecs.at[i], s.own_vecs.at[chip], s.sem_cv_s.at[i], s.sem_cv_r.at[chip], owner).wait_send()

    @pl.when(chip // half == core)
    def _():
        for z in range(chips):

            @pl.when(z != chip)
            def _():
                remote(s.back_send.at[z], s.back_vecs.at[mine], s.sem_bk_s.at[z], s.sem_bk_r.at[mine], 2 * z + core).wait_send()


def fourier_table(planes):
    row = np.arange(planes)[:, None]
    angles = (row // 2 * np.arange(planes)[None, :] % planes) * (2.0 * math.pi / planes)
    return (np.where(row % 2 == 0, np.cos(angles), -np.sin(angles)) / math.sqrt(planes)).astype(np.float32)


VMEM = pl.BlockSpec(memory_space=pltpu.VMEM)
SMEM = pl.BlockSpec(memory_space=pltpu.SMEM)
HBM = pl.BlockSpec(memory_space=pltpu.HBM)
LOADED = ("rhs", "table", "panel", "band", "radial", "stiff", "mass")


def body(
    rhs_phys,
    radial_basis,
    axial_basis,
    radial_eig,
    axial_eig,
    face_stiff,
    face_mass,
    axial_coupling,
    face_numbering,
    band_panels,
    inverse_panels,
):
    planes = rhs_phys.shape[0]
    mode_dev, slabs, n = inverse_panels.shape[:3]
    inner = axial_basis.shape[1]
    mode_axis = lax.axis_size("mode")
    chips = lax.axis_size("elem") // 2
    mode_total = mode_dev * mode_axis
    rows = 2 * mode_dev
    half = mode_dev // 2
    parts = half // max(half // 2, 1)
    width = rhs_phys.shape[1]

    table = fourier_table(planes)
    table_high = table.astype(ml_dtypes.bfloat16)
    table = np.stack([table_high, (table - table_high.astype(np.float32)).astype(ml_dtypes.bfloat16)])
    loaded = (rhs_phys, jnp.asarray(table), inverse_panels, band_panels, radial_basis, face_stiff, face_mass)

    def V(*shape, dtype=F32):
        return pltpu.VMEM(shape, dtype)

    def D(*shape):
        return pltpu.SemaphoreType.DMA(shape)

    scratch = {name: V(*array.shape, dtype=array.dtype) for name, array in zip(LOADED, loaded)}
    scratch.update(
        rs=V(slabs, 2, n, n, dtype=BF16),
        rts=V(slabs, 2, n, n, dtype=BF16),
        push=V(slabs, 2, 2, 2 * n, n, dtype=BF16),
        lift=V(slabs, 2, 2, 2 * n, n, dtype=BF16),
        es=V(slabs - 1, 2, 2 * n, n, dtype=BF16),
        ets=V(slabs - 1, 2, 2 * n, n, dtype=BF16),
        maps=V(mode_dev, 3, n, n),
        pts=V(mode_dev, slabs, 2, n, n, dtype=BF16),
        uts=V(mode_dev, slabs, 2, n, n, dtype=BF16),
        nts=V(mode_dev, slabs, 2, n, n, dtype=BF16),
        spec_out=V(mode_axis, rows, width),
        spec_in=V(mode_axis, rows, width),
        placed_in=V(rows, n),
        x_in=V(rows, n),
        x_send=V(rows, n),
        push_send=V(rows, n),
        pair_maps=V(2, half, 3, n, n),
        chip_maps=V(half, 3, n, n),
        own_maps=V(chips, 3, n, n),
        vec_send=V(mode_dev, 8, n),
        pair_vecs=V(2, half, 8, n),
        chip_vecs=V(half, 8, n),
        own_vecs=V(chips, 8, n),
        back_send=V(chips, 8, n),
        back_vecs=V(half, 8, n),
        fin_send=V(half, 8, n),
        fin=V(mode_dev, 8, n),
        sem_in=D(len(LOADED)),
        sem_sp=D(2),
        sem_pm_s=D(parts),
        sem_pm_r=D(parts),
        sem_cm_s=D(half, 2),
        sem_cm_r=D(chips, 2),
        sem_pl=D(2),
        sem_pv=D(2),
        sem_cv_s=D(half),
        sem_cv_r=D(chips),
        sem_bk_s=D(chips),
        sem_bk_r=D(half),
        sem_fn=D(2),
        sem_x=D(2),
    )
    names = [name + "_hbm" for name in LOADED] + ["out"] + list(scratch)
    return pl.pallas_call(
        functools.partial(solve_kernel, names, mode_axis, mode_dev, mode_total, chips),
        out_shape=jax.ShapeDtypeStruct((rows, slabs * (inner + 1) * n), F32),
        in_specs=[SMEM] * 3 + [VMEM] * 2 + [HBM] * len(LOADED),
        out_specs=VMEM,
        scratch_shapes=list(scratch.values()),
        compiler_params=pltpu.CompilerParams(
            collective_id=0, has_side_effects=True, vmem_limit_bytes=56 << 20
        ),
        name="pressure_solve",
    )(
        axial_basis.reshape(slabs * inner, inner),
        axial_coupling.reshape(2 * slabs, inner),
        axial_eig,
        radial_eig,
        face_numbering.reshape(2 * slabs, n),
        *loaded,
    )


def solution(mesh):
    placed = (
        P(None, ("elem", "mode")),
        P("elem", None, None),
        P("elem", None, None),
        P("elem", None),
        P("elem", None),
        P("elem", None, None),
        P("elem", None, None),
        P("elem", None, None),
        P("elem", None, None),
        P(None, "elem", None, None),
        P("mode", "elem", None, None),
    )
    return jax.shard_map(
        body, mesh=mesh, in_specs=placed, out_specs=P("mode", "elem"), check_vma=False
    )
```

```python
import functools
import math
from types import SimpleNamespace

import jax
import jax.numpy as jnp
import ml_dtypes
import numpy as np
from jax import lax
from jax.experimental import pallas as pl
from jax.experimental.pallas import tpu as pltpu
from jax.sharding import PartitionSpec as P

F32 = jnp.float32
BF16 = jnp.bfloat16


def split(x):
    hi = x.astype(BF16)
    return hi, (x - hi.astype(F32)).astype(BF16)


def bdot(a, b):
    return jnp.dot(a, b, preferred_element_type=F32)


def bdot_turned(a, b):
    return lax.dot_general(a, b, (((1,), (1,)), ((), ())), preferred_element_type=F32)


def mul_split(v, hi, lo):
    vh, vl = split(v)
    return bdot(vh, hi) + (bdot(vl, hi) + bdot(vh, lo))


def mul(a, b):
    return mul_split(a, *split(b))


def wave_square(index, mode_total):
    wave = index.astype(F32) / mode_total
    return 4.0 * wave * wave


def store_split(ref, at, x):
    hi, lo = split(x)
    ref[at + (0,)] = hi
    ref[at + (1,)] = lo


def slab_matrices(s, number_ref):
    slabs, n = s.radial.shape[0], s.radial.shape[1]
    turned = []
    for j in range(slabs):
        basis = s.radial[j]
        store_split(s.rs, (j,), basis)
        store_split(s.rts, (j,), basis.T)
        for face in (s.stiff, s.mass):
            turned.append(split(mul(face[j].T, basis)))
    for j in range(slabs):
        for side in range(2):
            numbers = number_ref[j, side : side + 1, :]
            hot = (lax.broadcasted_iota(jnp.int32, (n, n), 0) == numbers).astype(F32).astype(BF16)
            for part in range(2):
                th, tl = turned[2 * j + part]
                kt = bdot(hot, th) + bdot(hot, tl)
                for ref, x in ((s.lift, kt), (s.push, kt.T)):
                    hi, lo = split(x)
                    ref[j, side, 0, part * n : (part + 1) * n, :] = hi
                    ref[j, side, 1, part * n : (part + 1) * n, :] = lo
    for j in range(1, slabs):
        for part in range(2):
            band = s.band[part, j]
            for ref, x in ((s.es, band), (s.ets, band.T)):
                hi, lo = split(x)
                ref[j - 1, 0, part * n : (part + 1) * n, :] = hi
                ref[j - 1, 1, part * n : (part + 1) * n, :] = lo


def times(a, b):
    return bdot(a[0], b[0]) + (bdot(a[1], b[0]) + bdot(a[0], b[1]))


def mode_maps(s, core, modes, first, mode_total):
    slabs = s.panel.shape[1]
    count = len(modes)
    turned = [[s.band[p, j].T for p in range(2)] for j in range(slabs)]
    lams = [wave_square(first + m, mode_total) for m in modes]
    es = [[split(s.band[0, j] + lam * s.band[1, j]) for j in range(slabs)] for lam in lams]
    ets = [[split(turned[j][0] + lam * turned[j][1]) for j in range(slabs)] for lam in lams]
    pts = [[split(s.panel[m, j].T) for j in range(slabs)] for m in modes]
    for i, m in enumerate(modes):
        for j in range(slabs):
            s.pts[m, j, 0] = pts[i][j][0]
            s.pts[m, j, 1] = pts[i][j][1]
    ahead = [ets[i][0] for i in range(count)]
    back = [es[i][0] for i in range(count)]
    cross = [None] * count
    nears = [[] for _ in modes]
    for j in range(slabs):
        if j > 0:
            for i in range(count):
                ahead[i] = split(times(ahead[i], ets[i][j]))
                back[i] = split(times(es[i][j], back[i]))
        for i, m in enumerate(modes):
            s.uts[m, j, 0] = back[i][0]
            s.uts[m, j, 1] = back[i][1]
            full = -times(ahead[i], pts[i][j])
            ahead[i] = split(full)
            s.nts[m, j, 0] = ahead[i][0]
            s.nts[m, j, 1] = ahead[i][1]
            nears[i].append((ahead[i], back[i]))
            backed = -times(pts[i][j], back[i])
            back[i] = split(backed)
            if j == slabs - 1:
                s.both[core, m, 0] = full
                s.both[core, m, 1] = backed
    for j in range(slabs):
        for i in range(count):
            term = times(*nears[i][j])
            cross[i] = term if cross[i] is None else cross[i] + term
    for i, m in enumerate(modes):
        s.both[core, m, 2] = cross[i]


def solve_kernel(
    names,
    mode_axis,
    mode_dev,
    mode_total,
    chips,
    axial_ref,
    couple_ref,
    axial_eig_ref,
    radial_eig_ref,
    number_ref,
    *refs,
):
    s = SimpleNamespace(**dict(zip(names, refs)))
    out_ref = s.out
    slabs, n = s.rs.shape[0], s.rs.shape[-1]
    rows = 2 * mode_dev
    half = mode_dev // 2
    inner = axial_ref.shape[1]
    me = lax.axis_index("elem")
    count = 2 * chips
    core = lax.rem(me, 2)
    chip = me // 2
    other = 1 - core
    partner = 2 * chip + other

    fetch = []
    for at, name in enumerate(LOADED):
        copy = pltpu.make_async_copy(getattr(s, name + "_hbm"), getattr(s, name), s.sem_in.at[at])
        copy.start()
        fetch.append(copy)

    barrier = pltpu.get_barrier_semaphore()
    line = lax.axis_index("mode")
    for k in range(1, mode_axis):
        pl.semaphore_signal(barrier, 1, device_id={"mode": lax.rem(line + k, mode_axis)})
    for k in range(1, count):
        pl.semaphore_signal(barrier, 1, device_id={"elem": lax.rem(me + k, count)})

    def remote(src, dst, send, recv, device):
        return pltpu.make_async_remote_copy(
            src, dst, send, recv, device_id={"elem": device}, device_id_type=pl.DeviceIdType.MESH
        )

    row = lax.broadcasted_iota(jnp.int32, (rows, n), 0)
    lam = wave_square(lax.axis_index("mode") * mode_dev + row // 2, mode_total)

    def banded(v, ref):
        return mul_split(jnp.concatenate([v, lam * v], axis=1), ref[0], ref[1])

    def per_mode(v, ref, *at):
        vh, vl = split(v)
        both = jnp.concatenate([vh, vl], axis=0)
        sides = lax.broadcasted_iota(jnp.int32, (2 * rows, n), 0)
        sides = jnp.where(sides < rows, sides, sides - rows) // 2
        zero = jnp.zeros_like(both)
        total = None
        low = None
        for m in range(mode_dev):
            mine = jnp.where(sides == m, both, zero)
            term = bdot(mine, ref[(m,) + at + (0,)])
            term_low = bdot(mine[:rows], ref[(m,) + at + (1,)])
            total = term if total is None else total + term
            low = term_low if low is None else low + term_low
        return total[:rows] + (total[rows:] + low)

    for copy in fetch[:2]:
        copy.wait()
    first = line * mode_dev
    quarter = max(half // 2, 1)
    parts = [range(at, min(at + quarter, half)) for at in range(0, half, quarter)]
    shares = [[], []]
    for at, part in enumerate(parts):
        modes = [half * other + i for i in part] + [half * core + i for i in part]
        mode_maps(s, core, modes, first, mode_total)
        if at == 0:
            pl.semaphore_wait(barrier, mode_axis - 1 + count - 1)
        for whose, taken in ((other, 0), (core, 1)):
            block = s.both.at[core, pl.ds(half * whose + part[0], len(part))]
            share = remote(block, block, s.sem_pm_s.at[taken, at], s.sem_pm_r.at[taken, at], partner)
            share.start()
            shares[taken].append(share)

    for copy in fetch[2:4]:
        copy.wait()
    rhs = split(s.rhs[...])
    spectrum = bdot_turned(s.table[0], rhs[0]) + (bdot_turned(s.table[1], rhs[0]) + bdot_turned(s.table[0], rhs[1]))
    s.spec_out[...] = spectrum.reshape(s.spec_out.shape)

    def spread_out(k, carry):
        to = lax.rem(line + k, mode_axis)
        pltpu.make_async_remote_copy(
            s.spec_out.at[to],
            s.spec_in.at[line],
            s.sem_sp.at[0],
            s.sem_sp.at[1],
            device_id={"mode": to},
            device_id_type=pl.DeviceIdType.MESH,
        ).start()
        return carry

    lax.fori_loop(1, mode_axis, spread_out, 0)
    s.spec_in[line] = s.spec_out[line]


    def send_map(i, start):
        owner = half * core + i
        away = jnp.logical_and(owner != chip, chip > 0)
        to = 2 * owner + core
        ends = remote(
            s.chip_maps.at[i, pl.ds(0, 2)],
            s.own_maps.at[chip, pl.ds(0, 2)],
            s.sem_cm_s.at[i, 0],
            s.sem_cm_r.at[chip, 0],
            to,
        )
        cross = remote(
            s.chip_maps.at[i, 2], s.own_maps.at[chip, 2], s.sem_cm_s.at[i, 1], s.sem_cm_r.at[chip, 1], to
        )

        @pl.when(jnp.logical_and(away, chip < chips - 1))
        def _():
            ends.start() if start else ends.wait_send()

        @pl.when(away)
        def _():
            cross.start() if start else cross.wait_send()

    for part, share in zip(parts, shares[0]):
        share.wait()
        pair = [[[split(s.both[c, half * core + i, k]) for k in range(3)] for c in range(2)] for i in part]
        ahead = [times(one[0][0], one[1][0]) for one in pair]
        back = [times(one[1][1], one[0][1]) for one in pair]
        cross = [split(times(one[0][0], one[1][2])) for one in pair]
        cross = [times(x, one[0][1]) for x, one in zip(cross, pair)]
        for at, i in enumerate(part):
            s.chip_maps[i, 0] = ahead[at]
            s.chip_maps[i, 1] = back[at]
            s.chip_maps[i, 2] = s.both[0, half * core + i, 2] + cross[at]
        for i in part:
            send_map(i, True)

            @pl.when(half * core + i == chip)
            def _():
                s.own_maps[chip] = s.chip_maps[i]

    for copy in fetch[4:]:
        copy.wait()
    slab_matrices(s, number_ref)

    others = s.spec_in.at[pl.ds(0, mode_axis - 1)]
    pltpu.make_async_remote_copy(
        others, others, s.sem_sp.at[0], s.sem_sp.at[1], device_id={"mode": line}, device_id_type=pl.DeviceIdType.MESH
    ).wait()
    width = s.spec_in.shape[2]
    modal = []
    for t in range(slabs * (inner + 1)):
        pieces = []
        at = t * n
        while at < (t + 1) * n:
            source = at // width
            stop = min((t + 1) * n, (source + 1) * width)
            pieces.append(s.spec_in[source, :, at - source * width : stop - source * width])
            at = stop
        modal.append(pieces[0] if len(pieces) == 1 else jnp.concatenate(pieces, axis=1))

    spectral = []
    inverses = []
    sums = []
    fields = []
    for j in range(slabs):
        base = j * (inner + 1)
        x = jnp.concatenate([modal[base + a] for a in range(inner)], axis=0)
        fields.append(mul_split(x, s.rs[j, 0], s.rs[j, 1]))
    for j in range(slabs):
        x = fields[j]
        values = []
        scales = []
        for b in range(inner):
            total = x[:rows] * axial_ref[j, 0, b]
            for a in range(1, inner):
                total = total + x[a * rows : (a + 1) * rows] * axial_ref[j, a, b]
            scale = 1.0 / (axial_eig_ref[j, b] + radial_eig_ref[j : j + 1, :] + lam)
            scales.append(scale)
            values.append(total * scale)
        spectral.append(values)
        inverses.append(scales)
        faces = [None, None]
        for a in range(inner):
            total = values[0] * axial_ref[j, a, 0]
            for b in range(1, inner):
                total = total + values[b] * axial_ref[j, a, b]
            for side in range(2):
                term = total * couple_ref[j, side, a]
                faces[side] = term if faces[side] is None else faces[side] + term
        sums.append(faces)
        if j == 0:
            s.push_send[...] = banded(faces[0], s.push.at[0, 0])

            @pl.when(me > 0)
            def _():
                remote(s.push_send, s.placed_in, s.sem_pl.at[0], s.sem_pl.at[1], me - 1).start()

    placed = [
        [None if j + side == 0 else banded(sums[j][side], s.push.at[j, side]) for side in range(2)]
        for j in range(slabs)
    ]

    loads = [modal[j * (inner + 1) + inner] - placed[j][1] for j in range(slabs)]
    for j in range(slabs - 1):
        loads[j] = loads[j] - placed[j + 1][0]
    local = [per_mode(loads[0], s.pts, 0)]
    for j in range(1, slabs):
        load = loads[j] - banded(local[j - 1], s.ets.at[j - 1])
        if j == slabs - 1:

            @pl.when(me == count - 1)
            def _():
                s.placed_in[...] = jnp.zeros_like(s.placed_in)

            @pl.when(me < count - 1)
            def _():
                remote(s.push_send, s.placed_in, s.sem_pl.at[0], s.sem_pl.at[1], me).wait_recv()

            load = load - s.placed_in[...]
        local.append(per_mode(load, s.pts, j))
    offset = per_mode(local[0], s.uts, 0)
    for j in range(1, slabs):
        offset = offset + per_mode(local[j], s.uts, j)
    s.vec_send[...] = jnp.zeros_like(s.vec_send)
    for m in range(mode_dev):
        s.vec_send[m, 0:2, :] = local[-1][2 * m : 2 * m + 2]
        s.vec_send[m, 2:4, :] = offset[2 * m : 2 * m + 2]
    swap = remote(s.vec_send, s.mate_vecs, s.sem_pv.at[0], s.sem_pv.at[1], partner)
    swap.start()
    for share in shares[1]:
        share.wait()
    low = lax.broadcasted_iota(jnp.int32, (8, n), 0) < 2

    @pl.when(core == 0)
    def _():
        for m in range(mode_dev):
            tile = s.vec_send[m]
            turned = mul(mul(tile, s.both[1, m, 2]), s.both[0, m, 1])
            s.chip_vecs[m] = jnp.where(low, mul(tile, s.both[1, m, 0]), tile + pltpu.roll(turned, 2, 0))

    @pl.when(core == 1)
    def _():
        for m in range(mode_dev):
            tile = s.vec_send[m]
            s.chip_vecs[m] = jnp.where(low, tile, mul(tile, s.both[0, m, 1]))

    def vector_copy(m):
        return remote(
            s.chip_vecs.at[m],
            s.own_vecs.at[core, chip],
            s.sem_cv_s.at[m],
            s.sem_cv_r.at[core, chip],
            2 * m + m // half,
        )

    for m in range(mode_dev):

        @pl.when(me != 2 * m + m // half)
        def _():
            vector_copy(m).start()

        @pl.when(me == 2 * m + m // half)
        def _():
            s.own_vecs[core, chip] = s.chip_vecs[m]

    owner = chip // half == core

    @pl.when(owner)
    def _():
        for z in range(chips):
            for c in range(2):

                @pl.when(2 * z + c != me)
                def _():
                    remote(
                        s.chip_vecs.at[0], s.own_vecs.at[c, z], s.sem_cv_s.at[0], s.sem_cv_r.at[c, z], me
                    ).wait_recv()

            @pl.when(z != chip)
            def _():
                two = pl.ds(0, 2)
                if 0 < z < chips - 1:
                    remote(
                        s.chip_maps.at[0, two], s.own_maps.at[z, two], s.sem_cm_s.at[0, 0], s.sem_cm_r.at[z, 0], me
                    ).wait_recv()
                if z > 0:
                    remote(
                        s.chip_maps.at[0, 2], s.own_maps.at[z, 2], s.sem_cm_s.at[0, 1], s.sem_cm_r.at[z, 1], me
                    ).wait_recv()

        vecs = [s.own_vecs[0, z] + s.own_vecs[1, z] for z in range(chips)]
        state = jnp.zeros((8, n), F32)
        before = []
        terms = []
        for z in range(chips):
            before.append(state)
            if z > 0:
                terms.append(vecs[z] + pltpu.roll(mul(state, s.own_maps[z, 2]), 2, 0))
                if z < chips - 1:
                    state = mul(state, s.own_maps[z, 0]) + vecs[z]
            else:
                terms.append(vecs[z])
                state = vecs[z]
        state = jnp.zeros((8, n), F32)
        for z in reversed(range(chips)):
            s.back_send[z] = jnp.where(low, before[z], state)
            for c in range(2):

                @pl.when(2 * z + c != me)
                def _():
                    remote(
                        s.back_send.at[z],
                        s.back_vecs.at[chip],
                        s.sem_bk_s.at[z, c],
                        s.sem_bk_r.at[chip],
                        2 * z + c,
                    ).start()

            @pl.when(z == chip)
            def _():
                s.back_vecs[chip] = s.back_send[z]

            if z > 0:
                state = terms[z] if z == chips - 1 else mul(state, s.own_maps[z, 1]) + terms[z]

    swap.wait()
    for m in range(mode_dev):

        @pl.when(me != 2 * m + m // half)
        def _():
            remote(s.back_send.at[0], s.back_vecs.at[m], s.sem_bk_s.at[0, 0], s.sem_bk_r.at[m], me).wait_recv()

    @pl.when(core == 0)
    def _():
        for m in range(mode_dev):
            ends = s.back_vecs[m]
            middle = mul(ends, s.both[0, m, 0]) + s.vec_send[m]
            turned = mul(ends, s.both[1, m, 1]) + s.mate_vecs[m]
            s.fin[m] = jnp.where(low, ends, turned + pltpu.roll(mul(middle, s.both[1, m, 2]), 2, 0))

    @pl.when(core == 1)
    def _():
        for m in range(mode_dev):
            ends = s.back_vecs[m]
            s.fin[m] = jnp.where(low, mul(ends, s.both[0, m, 0]) + s.mate_vecs[m], ends)

    start = jnp.concatenate([s.fin[m, 0:2, :] for m in range(mode_dev)], axis=0)
    end = jnp.concatenate([s.fin[m, 2:4, :] for m in range(mode_dev)], axis=0)
    values = [None] * slabs
    for j in reversed(range(slabs)):
        full = local[j] + per_mode(start, s.nts, j)
        values[j] = full - per_mode(end, s.pts, j)
        if j == slabs - 1:
            s.x_send[...] = values[j]

            @pl.when(me < count - 1)
            def _():
                remote(s.x_send, s.x_in, s.sem_x.at[0], s.sem_x.at[1], me + 1).start()

        if j > 0:
            end = banded(values[j], s.es.at[j - 1])

    for j in reversed(range(slabs)):
        if j == 0:

            @pl.when(me == 0)
            def _():
                s.x_in[...] = jnp.zeros_like(s.x_in)

            @pl.when(me > 0)
            def _():
                remote(s.x_send, s.x_in, s.sem_x.at[0], s.sem_x.at[1], me).wait_recv()

            faces = [s.x_in[...], values[0]]
        else:
            faces = [values[j - 1], values[j]]
        lifted = [banded(faces[side], s.lift.at[j, side]) for side in range(2)]
        spread = [
            lifted[0] * couple_ref[j, 0, a] + lifted[1] * couple_ref[j, 1, a] for a in range(inner)
        ]
        left = []
        for b in range(inner):
            total = spread[0] * axial_ref[j, 0, b]
            for a in range(1, inner):
                total = total + spread[a] * axial_ref[j, a, b]
            left.append(spectral[j][b] - total * inverses[j][b])
        turned = []
        for a in range(inner):
            total = left[0] * axial_ref[j, a, 0]
            for b in range(1, inner):
                total = total + left[b] * axial_ref[j, a, b]
            turned.append(total)
        result = mul_split(jnp.concatenate(turned, axis=0), s.rts[j, 0], s.rts[j, 1])
        base = j * (inner + 1) * n
        for a in range(inner):
            out_ref[:, base + a * n : base + (a + 1) * n] = result[a * rows : (a + 1) * rows]
        out_ref[:, base + inner * n : base + (inner + 1) * n] = values[j]

    @pl.when(me > 0)
    def _():
        remote(s.push_send, s.placed_in, s.sem_pl.at[0], s.sem_pl.at[1], me - 1).wait_send()

    @pl.when(me < count - 1)
    def _():
        remote(s.x_send, s.x_in, s.sem_x.at[0], s.sem_x.at[1], me + 1).wait_send()

    for i in range(half):
        send_map(i, False)
    for m in range(mode_dev):

        @pl.when(me != 2 * m + m // half)
        def _():
            vector_copy(m).wait_send()

    @pl.when(owner)
    def _():
        for z in range(chips):
            for c in range(2):

                @pl.when(2 * z + c != me)
                def _():
                    remote(
                        s.back_send.at[z],
                        s.back_vecs.at[chip],
                        s.sem_bk_s.at[z, c],
                        s.sem_bk_r.at[chip],
                        2 * z + c,
                    ).wait_send()


def fourier_table(planes):
    row = np.arange(planes)[:, None]
    angles = (row // 2 * np.arange(planes)[None, :] % planes) * (2.0 * math.pi / planes)
    return (np.where(row % 2 == 0, np.cos(angles), -np.sin(angles)) / math.sqrt(planes)).astype(np.float32)


VMEM = pl.BlockSpec(memory_space=pltpu.VMEM)
SMEM = pl.BlockSpec(memory_space=pltpu.SMEM)
HBM = pl.BlockSpec(memory_space=pltpu.HBM)
LOADED = ("panel", "band", "rhs", "table", "radial", "stiff", "mass")


def body(
    rhs_phys,
    radial_basis,
    axial_basis,
    radial_eig,
    axial_eig,
    face_stiff,
    face_mass,
    axial_coupling,
    face_numbering,
    band_panels,
    inverse_panels,
):
    planes = rhs_phys.shape[0]
    mode_dev, slabs, n = inverse_panels.shape[:3]
    inner = axial_basis.shape[1]
    mode_axis = lax.axis_size("mode")
    chips = lax.axis_size("elem") // 2
    mode_total = mode_dev * mode_axis
    rows = 2 * mode_dev
    half = mode_dev // 2
    parts = half // max(half // 2, 1)
    width = rhs_phys.shape[1]

    table = fourier_table(planes)
    table_high = table.astype(ml_dtypes.bfloat16)
    table = np.stack([table_high, (table - table_high.astype(np.float32)).astype(ml_dtypes.bfloat16)])
    loaded = (inverse_panels, band_panels, rhs_phys.T, jnp.asarray(table), radial_basis, face_stiff, face_mass)

    def V(*shape, dtype=F32):
        return pltpu.VMEM(shape, dtype)

    def D(*shape):
        return pltpu.SemaphoreType.DMA(shape)

    scratch = {name: V(*array.shape, dtype=array.dtype) for name, array in zip(LOADED, loaded)}
    scratch.update(
        rs=V(slabs, 2, n, n, dtype=BF16),
        rts=V(slabs, 2, n, n, dtype=BF16),
        push=V(slabs, 2, 2, 2 * n, n, dtype=BF16),
        lift=V(slabs, 2, 2, 2 * n, n, dtype=BF16),
        es=V(slabs - 1, 2, 2 * n, n, dtype=BF16),
        ets=V(slabs - 1, 2, 2 * n, n, dtype=BF16),
        pts=V(mode_dev, slabs, 2, n, n, dtype=BF16),
        uts=V(mode_dev, slabs, 2, n, n, dtype=BF16),
        nts=V(mode_dev, slabs, 2, n, n, dtype=BF16),
        spec_out=V(mode_axis, rows, width),
        spec_in=V(mode_axis, rows, width),
        placed_in=V(rows, n),
        x_in=V(rows, n),
        x_send=V(rows, n),
        push_send=V(rows, n),
        both=V(2, mode_dev, 3, n, n),
        chip_maps=V(half, 3, n, n),
        own_maps=V(chips, 3, n, n),
        vec_send=V(mode_dev, 8, n),
        mate_vecs=V(mode_dev, 8, n),
        chip_vecs=V(mode_dev, 8, n),
        own_vecs=V(2, chips, 8, n),
        back_send=V(chips, 8, n),
        back_vecs=V(mode_dev, 8, n),
        fin=V(mode_dev, 8, n),
        sem_in=D(len(LOADED)),
        sem_sp=D(2),
        sem_pm_s=D(2, parts),
        sem_pm_r=D(2, parts),
        sem_cm_s=D(half, 2),
        sem_cm_r=D(chips, 2),
        sem_pl=D(2),
        sem_pv=D(2),
        sem_cv_s=D(mode_dev),
        sem_cv_r=D(2, chips),
        sem_bk_s=D(chips, 2),
        sem_bk_r=D(mode_dev),
        sem_x=D(2),
    )
    names = [name + "_hbm" for name in LOADED] + ["out"] + list(scratch)
    return pl.pallas_call(
        functools.partial(solve_kernel, names, mode_axis, mode_dev, mode_total, chips),
        out_shape=jax.ShapeDtypeStruct((rows, slabs * (inner + 1) * n), F32),
        in_specs=[SMEM] * 3 + [VMEM] * 2 + [HBM] * len(LOADED),
        out_specs=VMEM,
        scratch_shapes=list(scratch.values()),
        compiler_params=pltpu.CompilerParams(
            collective_id=0, has_side_effects=True, vmem_limit_bytes=56 << 20
        ),
        name="pressure_solve",
    )(
        axial_basis,
        axial_coupling,
        axial_eig,
        radial_eig,
        face_numbering,
        *loaded,
    )


def solution(mesh):
    placed = (
        P(None, ("elem", "mode")),
        P("elem", None, None),
        P("elem", None, None),
        P("elem", None),
        P("elem", None),
        P("elem", None, None),
        P("elem", None, None),
        P("elem", None, None),
        P("elem", None, None),
        P(None, "elem", None, None),
        P("mode", "elem", None, None),
    )
    return jax.shard_map(
        body, mesh=mesh, in_specs=placed, out_specs=P("mode", "elem"), check_vma=False
    )
```

```python
import functools
import math
from types import SimpleNamespace

import jax
import jax.numpy as jnp
import ml_dtypes
import numpy as np
from jax import lax
from jax.experimental import pallas as pl
from jax.experimental.pallas import tpu as pltpu
from jax.sharding import PartitionSpec as P

F32 = jnp.float32
BF16 = jnp.bfloat16


def split(x):
    hi = x.astype(BF16)
    return hi, (x - hi.astype(F32)).astype(BF16)


def bdot(a, b):
    return jnp.dot(a, b, preferred_element_type=F32)


def bdot_turned(a, b):
    return lax.dot_general(a, b, (((1,), (1,)), ((), ())), preferred_element_type=F32)


def mul_split(v, hi, lo):
    vh, vl = split(v)
    return bdot(vh, hi) + (bdot(vl, hi) + bdot(vh, lo))


def mul(a, b):
    return mul_split(a, *split(b))


def wave_square(index, mode_total):
    wave = index.astype(F32) / mode_total
    return 4.0 * wave * wave


def store_split(ref, at, x):
    hi, lo = split(x)
    ref[at + (0,)] = hi
    ref[at + (1,)] = lo


def slab_matrices(s, number_ref):
    slabs, n = s.radial.shape[0], s.radial.shape[1]
    turned = []
    for j in range(slabs):
        basis = s.radial[j]
        store_split(s.rs, (j,), basis)
        store_split(s.rts, (j,), basis.T)
        for face in (s.stiff, s.mass):
            turned.append(split(mul(face[j].T, basis)))
    for j in range(slabs):
        for side in range(2):
            numbers = number_ref[j, side : side + 1, :]
            hot = (lax.broadcasted_iota(jnp.int32, (n, n), 0) == numbers).astype(F32).astype(BF16)
            for part in range(2):
                th, tl = turned[2 * j + part]
                kt = bdot(hot, th) + bdot(hot, tl)
                for ref, x in ((s.lift, kt), (s.push, kt.T)):
                    hi, lo = split(x)
                    ref[j, side, 0, part * n : (part + 1) * n, :] = hi
                    ref[j, side, 1, part * n : (part + 1) * n, :] = lo
    for j in range(1, slabs):
        for part in range(2):
            band = s.band[part, j]
            for ref, x in ((s.es, band), (s.ets, band.T)):
                hi, lo = split(x)
                ref[j - 1, 0, part * n : (part + 1) * n, :] = hi
                ref[j - 1, 1, part * n : (part + 1) * n, :] = lo


def times(a, b):
    return bdot(a[0], b[0]) + (bdot(a[1], b[0]) + bdot(a[0], b[1]))


def mode_maps(s, core, modes, first, mode_total):
    slabs = s.panel.shape[1]
    count = len(modes)
    turned = [[s.band[p, j].T for p in range(2)] for j in range(slabs)]
    lams = [wave_square(first + m, mode_total) for m in modes]
    es = [[split(s.band[0, j] + lam * s.band[1, j]) for j in range(slabs)] for lam in lams]
    ets = [[split(turned[j][0] + lam * turned[j][1]) for j in range(slabs)] for lam in lams]
    pts = [[split(s.panel[m, j].T) for j in range(slabs)] for m in modes]
    for i, m in enumerate(modes):
        for j in range(slabs):
            s.pts[m, j, 0] = pts[i][j][0]
            s.pts[m, j, 1] = pts[i][j][1]
    ahead = [ets[i][0] for i in range(count)]
    back = [es[i][0] for i in range(count)]
    cross = [None] * count
    nears = [[] for _ in modes]
    for j in range(slabs):
        if j > 0:
            for i in range(count):
                ahead[i] = split(times(ahead[i], ets[i][j]))
                back[i] = split(times(es[i][j], back[i]))
        for i, m in enumerate(modes):
            s.uts[m, j, 0] = back[i][0]
            s.uts[m, j, 1] = back[i][1]
            full = -times(ahead[i], pts[i][j])
            ahead[i] = split(full)
            s.nts[m, j, 0] = ahead[i][0]
            s.nts[m, j, 1] = ahead[i][1]
            nears[i].append((ahead[i], back[i]))
            backed = -times(pts[i][j], back[i])
            back[i] = split(backed)
            if j == slabs - 1:
                s.both[core, m, 0] = full
                s.both[core, m, 1] = backed
    for j in range(slabs):
        for i in range(count):
            term = times(*nears[i][j])
            cross[i] = term if cross[i] is None else cross[i] + term
    for i, m in enumerate(modes):
        s.both[core, m, 2] = cross[i]


def last_maps(s, core, modes, first, mode_total):
    slabs, n = s.panel.shape[1], s.panel.shape[2]
    where = range(len(modes))
    lams = [wave_square(first + m, mode_total) for m in modes]
    bands = [[split(s.band[0, j] + lam * s.band[1, j]) for j in range(1, slabs)] for lam in lams]
    turns = [[times(bands[i][j], (s.pts[m, j, 0], s.pts[m, j, 1])) for j in range(slabs - 1)] for i, m in enumerate(modes)]
    turns = [[split(x) for x in row] for row in turns]
    near = [[None] * slabs for _ in modes]
    far = [[None] * slabs for _ in modes]
    for i, m in enumerate(modes):
        last = slabs - 1
        near[i][last] = (s.nts[m, last, 0], s.nts[m, last, 1])
        far[i][last] = (-s.pts[m, last, 0], -s.pts[m, last, 1])
    for j in reversed(range(slabs - 1)):
        for i, m in enumerate(modes):
            here = s.nts[m, j, 0].astype(F32) + s.nts[m, j, 1].astype(F32)
            near[i][j] = split(here - times(near[i][j + 1], turns[i][j]))
            far[i][j] = split(-times(far[i][j + 1], turns[i][j]))

    @pl.when(core == 0)
    def _():
        outer = [split(s.both[1, m, 1]) for m in modes]
        cross = [split(mul(s.both[0, m, 0], s.both[1, m, 2])) for m in modes]
        for j in range(slabs):
            for i, m in enumerate(modes):
                whole = near[i][j][0].astype(F32) + near[i][j][1].astype(F32)
                starts = split(whole + times(cross[i], far[i][j]))
                ends = split(times(outer[i], far[i][j]))
                for part in range(2):
                    s.last[m, j, part, 0:n] = starts[part]
                    s.last[m, j, part, n : 2 * n] = ends[part]
                    s.extra[m, j, part] = far[i][j][part]

    @pl.when(core == 1)
    def _():
        inner = [split(s.both[0, m, 0]) for m in modes]
        for j in range(slabs):
            for i, m in enumerate(modes):
                starts = split(times(inner[i], near[i][j]))
                for part in range(2):
                    s.last[m, j, part, 0:n] = starts[part]
                    s.last[m, j, part, n : 2 * n] = far[i][j][part]
                    s.extra[m, j, part] = near[i][j][part]


def solve_kernel(
    names,
    mode_axis,
    mode_dev,
    mode_total,
    chips,
    axial_ref,
    couple_ref,
    axial_eig_ref,
    radial_eig_ref,
    number_ref,
    *refs,
):
    s = SimpleNamespace(**dict(zip(names, refs)))
    out_ref = s.out
    slabs, n = s.rs.shape[0], s.rs.shape[-1]
    rows = 2 * mode_dev
    half = mode_dev // 2
    inner = axial_ref.shape[1]
    me = lax.axis_index("elem")
    count = 2 * chips
    core = lax.rem(me, 2)
    chip = me // 2
    other = 1 - core
    partner = 2 * chip + other

    parts = [[lax.rem(chip + k, half)] for k in range(half)]
    fetch = {}
    for at, name in enumerate(LOADED[1:]):
        copy = pltpu.make_async_copy(getattr(s, name + "_hbm"), getattr(s, name), s.sem_in.at[at])
        copy.start()
        fetch[name] = copy
        if at == 0:
            panels = []
            for k, part in enumerate(parts):
                for j, whose in enumerate((other, core)):
                    block = pl.ds(half * whose + part[0], len(part))
                    copy = pltpu.make_async_copy(s.panel_hbm.at[block], s.panel.at[block], s.sem_pa.at[k, j])
                    copy.start()
                    panels.append(copy)

    barrier = pltpu.get_barrier_semaphore()
    line = lax.axis_index("mode")
    for k in range(1, mode_axis):
        pl.semaphore_signal(barrier, 1, device_id={"mode": lax.rem(line + k, mode_axis)})
    for k in range(1, count):
        pl.semaphore_signal(barrier, 1, device_id={"elem": lax.rem(me + k, count)})

    def remote(src, dst, send, recv, device):
        return pltpu.make_async_remote_copy(
            src, dst, send, recv, device_id={"elem": device}, device_id_type=pl.DeviceIdType.MESH
        )

    row = lax.broadcasted_iota(jnp.int32, (rows, n), 0)
    lam = wave_square(lax.axis_index("mode") * mode_dev + row // 2, mode_total)

    def banded(v, ref):
        return mul_split(jnp.concatenate([v, lam * v], axis=1), ref[0], ref[1])

    def per_mode(v, ref, *at):
        vh, vl = split(v)
        both = jnp.concatenate([vh, vl], axis=0)
        sides = lax.broadcasted_iota(jnp.int32, both.shape, 0)
        sides = jnp.where(sides < rows, sides, sides - rows) // 2
        zero = jnp.zeros_like(both)
        total = None
        low = None
        for m in range(mode_dev):
            mine = jnp.where(sides == m, both, zero)
            term = bdot(mine, ref[(m,) + at + (0,)])
            term_low = bdot(mine[:rows], ref[(m,) + at + (1,)])
            total = term if total is None else total + term
            low = term_low if low is None else low + term_low
        return total[:rows] + (total[rows:] + low)

    def send_map(i, k, start):
        owner = half * core + i
        away = jnp.logical_and(owner != chip, chip > 0)
        if k < 2:
            away = jnp.logical_and(away, chip < chips - 1)

        @pl.when(away)
        def _():
            copy = remote(
                s.chip_maps.at[i, k],
                s.own_maps.at[chip, k],
                s.sem_cm_s.at[i, k],
                s.sem_cm_r.at[chip, k],
                2 * owner + core,
            )
            copy.start() if start else copy.wait_send()

    def pairing(part, share):
        share.wait()
        pair = [[[split(s.both[c, half * core + i, k]) for k in range(3)] for c in range(2)] for i in part]
        ahead = [times(one[0][0], one[1][0]) for one in pair]
        back = [times(one[1][1], one[0][1]) for one in pair]
        cross = [split(times(one[0][0], one[1][2])) for one in pair]
        cross = [times(x, one[0][1]) for x, one in zip(cross, pair)]
        for at, i in enumerate(part):
            s.chip_maps[i, 0] = ahead[at]
            s.chip_maps[i, 1] = back[at]
            s.chip_maps[i, 2] = s.both[0, half * core + i, 2] + cross[at]
        for i in part:
            for k in (0, 2, 1):
                send_map(i, k, True)

            @pl.when(half * core + i == chip)
            def _():
                s.own_maps[chip] = s.chip_maps[i]

    fetch["band"].wait()
    first = line * mode_dev
    shares = [[], []]
    for at, part in enumerate(parts):
        modes = [half * other + i for i in part] + [half * core + i for i in part]
        for copy in panels[2 * at : 2 * at + 2]:
            copy.wait()
        mode_maps(s, core, modes, first, mode_total)
        if at == 0:
            pl.semaphore_wait(barrier, mode_axis - 1 + count - 1)
        for whose, taken in ((other, 0), (core, 1)):
            block = s.both.at[core, pl.ds(half * whose + part[0], len(part))]
            share = remote(block, block, s.sem_pm_s.at[taken, at], s.sem_pm_r.at[taken, at], partner)
            share.start()
            shares[taken].append(share)
        if at > 0:
            pairing(parts[at - 1], shares[0][at - 1])

    fetch["rhs"].wait()
    fetch["table"].wait()
    rhs = split(s.rhs[...])
    spectrum = bdot_turned(s.table[0], rhs[0]) + (bdot_turned(s.table[1], rhs[0]) + bdot_turned(s.table[0], rhs[1]))
    s.spec_out[...] = spectrum.reshape(s.spec_out.shape)

    def spread_out(k, carry):
        to = lax.rem(line + k, mode_axis)
        pltpu.make_async_remote_copy(
            s.spec_out.at[to],
            s.spec_in.at[line],
            s.sem_sp.at[0],
            s.sem_sp.at[1],
            device_id={"mode": to},
            device_id_type=pl.DeviceIdType.MESH,
        ).start()
        return carry

    lax.fori_loop(1, mode_axis, spread_out, 0)
    s.spec_in[line] = s.spec_out[line]

    pairing(parts[-1], shares[0][-1])
    for name in ("radial", "stiff", "mass"):
        fetch[name].wait()
    slab_matrices(s, number_ref)

    for share in shares[1]:
        share.wait()
    for at in range(0, mode_dev, half):
        last_maps(s, core, range(at, at + half), first, mode_total)

    others = s.spec_in.at[pl.ds(0, mode_axis - 1)]
    pltpu.make_async_remote_copy(
        others, others, s.sem_sp.at[0], s.sem_sp.at[1], device_id={"mode": line}, device_id_type=pl.DeviceIdType.MESH
    ).wait()
    width = s.spec_in.shape[2]
    modal = []
    for t in range(slabs * (inner + 1)):
        pieces = []
        at = t * n
        while at < (t + 1) * n:
            source = at // width
            stop = min((t + 1) * n, (source + 1) * width)
            pieces.append(s.spec_in[source, :, at - source * width : stop - source * width])
            at = stop
        modal.append(pieces[0] if len(pieces) == 1 else jnp.concatenate(pieces, axis=1))

    spectral = []
    inverses = []
    sums = []
    fields = []
    for j in range(slabs):
        base = j * (inner + 1)
        x = jnp.concatenate([modal[base + a] for a in range(inner)], axis=0)
        fields.append(mul_split(x, s.rs[j, 0], s.rs[j, 1]))
    for j in range(slabs):
        x = fields[j]
        values = []
        scales = []
        for b in range(inner):
            total = x[:rows] * axial_ref[j, 0, b]
            for a in range(1, inner):
                total = total + x[a * rows : (a + 1) * rows] * axial_ref[j, a, b]
            scale = 1.0 / (axial_eig_ref[j, b] + radial_eig_ref[j : j + 1, :] + lam)
            scales.append(scale)
            values.append(total * scale)
        spectral.append(values)
        inverses.append(scales)
        faces = [None, None]
        for a in range(inner):
            total = values[0] * axial_ref[j, a, 0]
            for b in range(1, inner):
                total = total + values[b] * axial_ref[j, a, b]
            for side in range(2):
                term = total * couple_ref[j, side, a]
                faces[side] = term if faces[side] is None else faces[side] + term
        sums.append(faces)
        if j == 0:
            s.push_send[...] = banded(faces[0], s.push.at[0, 0])

            @pl.when(me > 0)
            def _():
                remote(s.push_send, s.placed_in, s.sem_pl.at[0], s.sem_pl.at[1], me - 1).start()

    placed = [
        [None if j + side == 0 else banded(sums[j][side], s.push.at[j, side]) for side in range(2)]
        for j in range(slabs)
    ]

    loads = [modal[j * (inner + 1) + inner] - placed[j][1] for j in range(slabs)]
    for j in range(slabs - 1):
        loads[j] = loads[j] - placed[j + 1][0]
    local = [per_mode(loads[0], s.pts, 0)]
    for j in range(1, slabs):
        load = loads[j] - banded(local[j - 1], s.ets.at[j - 1])
        if j == slabs - 1:

            @pl.when(me == count - 1)
            def _():
                s.placed_in[...] = jnp.zeros_like(s.placed_in)

            @pl.when(me < count - 1)
            def _():
                remote(s.push_send, s.placed_in, s.sem_pl.at[0], s.sem_pl.at[1], me).wait_recv()

            load = load - s.placed_in[...]
        local.append(per_mode(load, s.pts, j))
    offset = per_mode(local[0], s.uts, 0)
    for j in range(1, slabs):
        offset = offset + per_mode(local[j], s.uts, j)
    s.vec_send[...] = jnp.zeros_like(s.vec_send)
    for m in range(mode_dev):
        s.vec_send[m, 0:2, :] = local[-1][2 * m : 2 * m + 2]
        s.vec_send[m, 2:4, :] = offset[2 * m : 2 * m + 2]
    swap = remote(s.vec_send, s.mate_vecs, s.sem_pv.at[0], s.sem_pv.at[1], partner)
    swap.start()
    low = lax.broadcasted_iota(jnp.int32, (8, n), 0) < 2

    @pl.when(core == 0)
    def _():
        for m in range(mode_dev):
            tile = s.vec_send[m]
            turned = mul(mul(tile, s.both[1, m, 2]), s.both[0, m, 1])
            s.chip_vecs[m] = jnp.where(low, mul(tile, s.both[1, m, 0]), tile + pltpu.roll(turned, 2, 0))

    @pl.when(core == 1)
    def _():
        for m in range(mode_dev):
            tile = s.vec_send[m]
            s.chip_vecs[m] = jnp.where(low, tile, mul(tile, s.both[0, m, 1]))

    is_owner = chip // half == core
    for m in range(mode_dev):
        to = 2 * m + m // half

        @pl.when(me != to)
        def _():
            remote(s.chip_vecs.at[m], s.own_vecs.at[me], s.sem_cv.at[0], s.sem_cv.at[1], to).start()

        @pl.when(me == to)
        def _():
            s.own_vecs[me] = s.chip_vecs[m]

    def tiles(ref, number, sems):
        block = ref.at[pl.ds(0, number)]
        return remote(block, block, sems.at[0], sems.at[1], me)

    local_values = [None] * slabs
    local_values[-1] = local[-1]
    for j in reversed(range(slabs - 1)):
        local_values[j] = local[j] - per_mode(banded(local_values[j + 1], s.es.at[j]), s.pts, j)
    swap.wait()

    @pl.when(core == 0)
    def _():
        for m in range(mode_dev):
            turned = s.mate_vecs[m] + pltpu.roll(mul(s.vec_send[m], s.both[1, m, 2]), 2, 0)
            s.fin[m] = pltpu.roll(turned, 6, 0)

    @pl.when(core == 1)
    def _():
        s.fin[...] = s.mate_vecs[...]

    within = jnp.concatenate([s.fin[m, 0:2, :] for m in range(mode_dev)], axis=0)
    for j in range(slabs):
        local_values[j] = local_values[j] + per_mode(within, s.extra, j)

    @pl.when(is_owner)
    def _():
        tiles(s.own_vecs, count - 1, s.sem_cv).wait_recv()

        def arrived(z, k):
            @pl.when(z != chip)
            def _():
                remote(
                    s.chip_maps.at[0, k], s.own_maps.at[z, k], s.sem_cm_s.at[0, k], s.sem_cm_r.at[z, k], me
                ).wait_recv()

        for z in range(1, chips - 1):
            arrived(z, 0)
        vecs = [s.own_vecs[2 * z] + s.own_vecs[2 * z + 1] for z in range(chips)]
        state = jnp.zeros((8, n), F32)
        before = []
        for z in range(chips):
            before.append(state)
            if z == 0:
                state = vecs[z]
            elif z < chips - 1:
                state = mul(state, s.own_maps[z, 0]) + vecs[z]
        for z in range(1, chips):
            arrived(z, 2)
            if z < chips - 1:
                arrived(z, 1)
        terms = [vecs[0]]
        for z in range(1, chips):
            terms.append(vecs[z] + pltpu.roll(mul(before[z], s.own_maps[z, 2]), 2, 0))
        state = jnp.zeros((8, n), F32)
        for z in reversed(range(chips)):
            back = jnp.where(low, before[z], state)
            s.back_send[2 * z] = back
            s.back_send[2 * z + 1] = back
            if z > 0:
                state = terms[z] if z == chips - 1 else mul(state, s.own_maps[z, 1]) + terms[z]

        def answer(k, carry):
            to = lax.rem(me + k, count)
            remote(s.back_send.at[to], s.back_vecs.at[chip], s.sem_bk.at[0], s.sem_bk.at[1], to).start()
            return carry

        lax.fori_loop(1, count, answer, 0, unroll=True)
        s.back_vecs[chip] = s.back_send[me]
        tiles(s.back_vecs, mode_dev - 1, s.sem_bk).wait_recv()

    @pl.when(jnp.logical_not(is_owner))
    def _():
        tiles(s.back_vecs, mode_dev, s.sem_bk).wait_recv()

    start = jnp.concatenate([s.back_vecs[m, 0:2, :] for m in range(mode_dev)], axis=0)
    end = jnp.concatenate([s.back_vecs[m, 2:4, :] for m in range(mode_dev)], axis=0)
    bounds = jnp.concatenate([start, end], axis=1)
    values = [None] * slabs
    for j in reversed(range(slabs)):
        values[j] = local_values[j] + per_mode(bounds, s.last, j)
        if j == slabs - 1:
            s.x_send[...] = values[j]

            @pl.when(me < count - 1)
            def _():
                remote(s.x_send, s.x_in, s.sem_x.at[0], s.sem_x.at[1], me + 1).start()

    for j in reversed(range(slabs)):
        if j == 0:
            for i in range(half):
                for k in range(3):
                    send_map(i, k, False)

            @pl.when(is_owner)
            def _():
                tiles(s.chip_vecs, mode_dev - 1, s.sem_cv).wait_send()

            @pl.when(jnp.logical_not(is_owner))
            def _():
                tiles(s.chip_vecs, mode_dev, s.sem_cv).wait_send()

            @pl.when(me == 0)
            def _():
                s.x_in[...] = jnp.zeros_like(s.x_in)

            @pl.when(me > 0)
            def _():
                remote(s.x_send, s.x_in, s.sem_x.at[0], s.sem_x.at[1], me).wait_recv()

            faces = [s.x_in[...], values[0]]
        else:
            faces = [values[j - 1], values[j]]
        lifted = [banded(faces[side], s.lift.at[j, side]) for side in range(2)]
        spread = [
            lifted[0] * couple_ref[j, 0, a] + lifted[1] * couple_ref[j, 1, a] for a in range(inner)
        ]
        left = []
        for b in range(inner):
            total = spread[0] * axial_ref[j, 0, b]
            for a in range(1, inner):
                total = total + spread[a] * axial_ref[j, a, b]
            left.append(spectral[j][b] - total * inverses[j][b])
        turned = []
        for a in range(inner):
            total = left[0] * axial_ref[j, a, 0]
            for b in range(1, inner):
                total = total + left[b] * axial_ref[j, a, b]
            turned.append(total)
        result = mul_split(jnp.concatenate(turned, axis=0), s.rts[j, 0], s.rts[j, 1])
        base = j * (inner + 1) * n
        for a in range(inner):
            out_ref[:, base + a * n : base + (a + 1) * n] = result[a * rows : (a + 1) * rows]
        out_ref[:, base + inner * n : base + (inner + 1) * n] = values[j]

    @pl.when(me > 0)
    def _():
        remote(s.push_send, s.placed_in, s.sem_pl.at[0], s.sem_pl.at[1], me - 1).wait_send()

    @pl.when(me < count - 1)
    def _():
        remote(s.x_send, s.x_in, s.sem_x.at[0], s.sem_x.at[1], me + 1).wait_send()

    @pl.when(is_owner)
    def _():
        tiles(s.back_send, count - 1, s.sem_bk).wait_send()


def fourier_table(planes):
    row = np.arange(planes)[:, None]
    angles = (row // 2 * np.arange(planes)[None, :] % planes) * (2.0 * math.pi / planes)
    return (np.where(row % 2 == 0, np.cos(angles), -np.sin(angles)) / math.sqrt(planes)).astype(np.float32)


VMEM = pl.BlockSpec(memory_space=pltpu.VMEM)
SMEM = pl.BlockSpec(memory_space=pltpu.SMEM)
HBM = pl.BlockSpec(memory_space=pltpu.HBM)
LOADED = ("panel", "band", "rhs", "table", "radial", "stiff", "mass")


def body(
    rhs_phys,
    radial_basis,
    axial_basis,
    radial_eig,
    axial_eig,
    face_stiff,
    face_mass,
    axial_coupling,
    face_numbering,
    band_panels,
    inverse_panels,
):
    planes = rhs_phys.shape[0]
    mode_dev, slabs, n = inverse_panels.shape[:3]
    inner = axial_basis.shape[1]
    mode_axis = lax.axis_size("mode")
    chips = lax.axis_size("elem") // 2
    mode_total = mode_dev * mode_axis
    rows = 2 * mode_dev
    half = mode_dev // 2
    parts = half
    count = 2 * chips
    width = rhs_phys.shape[1]

    table = fourier_table(planes)
    table_high = table.astype(ml_dtypes.bfloat16)
    table = np.stack([table_high, (table - table_high.astype(np.float32)).astype(ml_dtypes.bfloat16)])
    loaded = (inverse_panels, band_panels, rhs_phys.T, jnp.asarray(table), radial_basis, face_stiff, face_mass)

    def V(*shape, dtype=F32):
        return pltpu.VMEM(shape, dtype)

    def D(*shape):
        return pltpu.SemaphoreType.DMA(shape)

    scratch = {name: V(*array.shape, dtype=array.dtype) for name, array in zip(LOADED, loaded)}
    scratch.update(
        rs=V(slabs, 2, n, n, dtype=BF16),
        rts=V(slabs, 2, n, n, dtype=BF16),
        push=V(slabs, 2, 2, 2 * n, n, dtype=BF16),
        lift=V(slabs, 2, 2, 2 * n, n, dtype=BF16),
        es=V(slabs - 1, 2, 2 * n, n, dtype=BF16),
        ets=V(slabs - 1, 2, 2 * n, n, dtype=BF16),
        pts=V(mode_dev, slabs, 2, n, n, dtype=BF16),
        uts=V(mode_dev, slabs, 2, n, n, dtype=BF16),
        nts=V(mode_dev, slabs, 2, n, n, dtype=BF16),
        last=V(mode_dev, slabs, 2, 2 * n, n, dtype=BF16),
        extra=V(mode_dev, slabs, 2, n, n, dtype=BF16),
        spec_out=V(mode_axis, rows, width),
        spec_in=V(mode_axis, rows, width),
        placed_in=V(rows, n),
        x_in=V(rows, n),
        x_send=V(rows, n),
        push_send=V(rows, n),
        both=V(2, mode_dev, 3, n, n),
        chip_maps=V(half, 3, n, n),
        own_maps=V(chips, 3, n, n),
        vec_send=V(mode_dev, 8, n),
        mate_vecs=V(mode_dev, 8, n),
        chip_vecs=V(mode_dev, 8, n),
        own_vecs=V(count, 8, n),
        back_send=V(count, 8, n),
        back_vecs=V(mode_dev, 8, n),
        fin=V(mode_dev, 8, n),
        sem_in=D(len(LOADED) - 1),
        sem_pa=D(parts, 2),
        sem_sp=D(2),
        sem_pm_s=D(2, parts),
        sem_pm_r=D(2, parts),
        sem_cm_s=D(half, 3),
        sem_cm_r=D(chips, 3),
        sem_pl=D(2),
        sem_pv=D(2),
        sem_cv=D(2),
        sem_bk=D(2),
        sem_x=D(2),
    )
    names = [name + "_hbm" for name in LOADED] + ["out"] + list(scratch)
    return pl.pallas_call(
        functools.partial(solve_kernel, names, mode_axis, mode_dev, mode_total, chips),
        out_shape=jax.ShapeDtypeStruct((rows, slabs * (inner + 1) * n), F32),
        in_specs=[SMEM] * 3 + [VMEM] * 2 + [HBM] * len(LOADED),
        out_specs=VMEM,
        scratch_shapes=list(scratch.values()),
        compiler_params=pltpu.CompilerParams(
            collective_id=0, has_side_effects=True, vmem_limit_bytes=56 << 20
        ),
        name="pressure_solve",
    )(
        axial_basis,
        axial_coupling,
        axial_eig,
        radial_eig,
        face_numbering,
        *loaded,
    )


def solution(mesh):
    placed = (
        P(None, ("elem", "mode")),
        P("elem", None, None),
        P("elem", None, None),
        P("elem", None),
        P("elem", None),
        P("elem", None, None),
        P("elem", None, None),
        P("elem", None, None),
        P("elem", None, None),
        P(None, "elem", None, None),
        P("mode", "elem", None, None),
    )
    return jax.shard_map(
        body, mesh=mesh, in_specs=placed, out_specs=P("mode", "elem"), check_vma=False
    )
```

```python
import functools
import math
from types import SimpleNamespace

import jax
import jax.numpy as jnp
import ml_dtypes
import numpy as np
from jax import lax
from jax.experimental import pallas as pl
from jax.experimental.pallas import tpu as pltpu
from jax.sharding import PartitionSpec as P

F32 = jnp.float32
BF16 = jnp.bfloat16


def split(x):
    hi = x.astype(BF16)
    return hi, (x - hi.astype(F32)).astype(BF16)


def bdot(a, b):
    return jnp.dot(a, b, preferred_element_type=F32)


def bdot_turned(a, b):
    return lax.dot_general(a, b, (((1,), (1,)), ((), ())), preferred_element_type=F32)


def mul_split(v, hi, lo):
    vh, vl = split(v)
    return bdot(vh, hi) + (bdot(vl, hi) + bdot(vh, lo))


def mul(a, b):
    return mul_split(a, *split(b))


def wave_square(index, mode_total):
    wave = index.astype(F32) / mode_total
    return 4.0 * wave * wave


def store_split(ref, at, x):
    hi, lo = split(x)
    ref[at + (0,)] = hi
    ref[at + (1,)] = lo


def slab_matrices(s, number_ref):
    slabs, n = s.radial.shape[0], s.radial.shape[1]
    turned = []
    for j in range(slabs):
        basis = s.radial[j]
        store_split(s.rs, (j,), basis)
        store_split(s.rts, (j,), basis.T)
        for face in (s.stiff, s.mass):
            turned.append(split(mul(face[j].T, basis)))
    for j in range(slabs):
        for side in range(2):
            numbers = number_ref[j, side : side + 1, :]
            hot = (lax.broadcasted_iota(jnp.int32, (n, n), 0) == numbers).astype(F32).astype(BF16)
            for part in range(2):
                th, tl = turned[2 * j + part]
                kt = bdot(hot, th) + bdot(hot, tl)
                for ref, x in ((s.lift, kt), (s.push, kt.T)):
                    hi, lo = split(x)
                    ref[j, side, 0, part * n : (part + 1) * n, :] = hi
                    ref[j, side, 1, part * n : (part + 1) * n, :] = lo
    for j in range(1, slabs):
        for part in range(2):
            band = s.band[part, j]
            for ref, x in ((s.es, band), (s.ets, band.T)):
                hi, lo = split(x)
                ref[j - 1, 0, part * n : (part + 1) * n, :] = hi
                ref[j - 1, 1, part * n : (part + 1) * n, :] = lo


def times(a, b):
    return bdot(a[0], b[0]) + (bdot(a[1], b[0]) + bdot(a[0], b[1]))


def mode_maps(s, core, modes, first, mode_total):
    slabs = s.panel.shape[1]
    count = len(modes)
    turned = [[s.band[p, j].T for p in range(2)] for j in range(slabs)]
    lams = [wave_square(first + m, mode_total) for m in modes]
    es = [[split(s.band[0, j] + lam * s.band[1, j]) for j in range(slabs)] for lam in lams]
    ets = [[split(turned[j][0] + lam * turned[j][1]) for j in range(slabs)] for lam in lams]
    pts = [[split(s.panel[m, j].T) for j in range(slabs)] for m in modes]
    for i, m in enumerate(modes):
        for j in range(slabs):
            s.pts[m, j, 0] = pts[i][j][0]
            s.pts[m, j, 1] = pts[i][j][1]
    ahead = [ets[i][0] for i in range(count)]
    back = [es[i][0] for i in range(count)]
    cross = [None] * count
    nears = [[] for _ in modes]
    for j in range(slabs):
        if j > 0:
            for i in range(count):
                ahead[i] = split(times(ahead[i], ets[i][j]))
                back[i] = split(times(es[i][j], back[i]))
        for i, m in enumerate(modes):
            s.uts[m, j, 0] = back[i][0]
            s.uts[m, j, 1] = back[i][1]
            full = -times(ahead[i], pts[i][j])
            ahead[i] = split(full)
            s.nts[m, j, 0] = ahead[i][0]
            s.nts[m, j, 1] = ahead[i][1]
            nears[i].append((ahead[i], back[i]))
            backed = -times(pts[i][j], back[i])
            back[i] = split(backed)
            if j == slabs - 1:
                s.both[core, m, 0] = full
                s.both[core, m, 1] = backed
    for j in range(slabs):
        for i in range(count):
            term = times(*nears[i][j])
            cross[i] = term if cross[i] is None else cross[i] + term
    for i, m in enumerate(modes):
        s.both[core, m, 2] = cross[i]


def last_maps(s, core, modes, first, mode_total):
    slabs, n = s.panel.shape[1], s.panel.shape[2]
    where = range(len(modes))
    lams = [wave_square(first + m, mode_total) for m in modes]
    bands = [[split(s.band[0, j] + lam * s.band[1, j]) for j in range(1, slabs)] for lam in lams]
    turns = [[times(bands[i][j], (s.pts[m, j, 0], s.pts[m, j, 1])) for j in range(slabs - 1)] for i, m in enumerate(modes)]
    turns = [[split(x) for x in row] for row in turns]
    near = [[None] * slabs for _ in modes]
    far = [[None] * slabs for _ in modes]
    for i, m in enumerate(modes):
        last = slabs - 1
        near[i][last] = (s.nts[m, last, 0], s.nts[m, last, 1])
        far[i][last] = (-s.pts[m, last, 0], -s.pts[m, last, 1])
    for j in reversed(range(slabs - 1)):
        for i, m in enumerate(modes):
            here = s.nts[m, j, 0].astype(F32) + s.nts[m, j, 1].astype(F32)
            near[i][j] = split(here - times(near[i][j + 1], turns[i][j]))
            far[i][j] = split(-times(far[i][j + 1], turns[i][j]))

    @pl.when(core == 0)
    def _():
        outer = [split(s.both[1, m, 1]) for m in modes]
        cross = [split(mul(s.both[0, m, 0], s.both[1, m, 2])) for m in modes]
        for j in range(slabs):
            for i, m in enumerate(modes):
                whole = near[i][j][0].astype(F32) + near[i][j][1].astype(F32)
                starts = split(whole + times(cross[i], far[i][j]))
                ends = split(times(outer[i], far[i][j]))
                for part in range(2):
                    s.last[m, j, part, 0:n] = starts[part]
                    s.last[m, j, part, n : 2 * n] = ends[part]
                    s.extra[m, j, part] = far[i][j][part]

    @pl.when(core == 1)
    def _():
        inner = [split(s.both[0, m, 0]) for m in modes]
        for j in range(slabs):
            for i, m in enumerate(modes):
                starts = split(times(inner[i], near[i][j]))
                for part in range(2):
                    s.last[m, j, part, 0:n] = starts[part]
                    s.last[m, j, part, n : 2 * n] = far[i][j][part]
                    s.extra[m, j, part] = near[i][j][part]


def solve_kernel(
    names,
    mode_axis,
    mode_dev,
    mode_total,
    chips,
    axial_ref,
    couple_ref,
    axial_eig_ref,
    radial_eig_ref,
    number_ref,
    *refs,
):
    s = SimpleNamespace(**dict(zip(names, refs)))
    out_ref = s.out
    slabs, n = s.rs.shape[0], s.rs.shape[-1]
    rows = 2 * mode_dev
    half = mode_dev // 2
    inner = axial_ref.shape[1]
    me = lax.axis_index("elem")
    count = 2 * chips
    core = lax.rem(me, 2)
    chip = me // 2
    other = 1 - core
    partner = 2 * chip + other


    def turn(k):
        return lax.rem(chip + k, half)

    def panel_copy(k, side):
        block = pl.ds(half * jnp.where(side == 0, other, core) + turn(k), 1)
        return pltpu.make_async_copy(s.panel_hbm.at[block], s.panel.at[block], s.sem_pa.at[k, side])

    fetch = {}
    for at, name in enumerate(LOADED[1:]):
        copy = pltpu.make_async_copy(getattr(s, name + "_hbm"), getattr(s, name), s.sem_in.at[at])
        copy.start()
        fetch[name] = copy
        if at == 0:
            for k in range(half):
                for side in range(2):
                    panel_copy(k, side).start()

    barrier = pltpu.get_barrier_semaphore()
    line = lax.axis_index("mode")
    for k in range(1, mode_axis):
        pl.semaphore_signal(barrier, 1, device_id={"mode": lax.rem(line + k, mode_axis)})
    for k in range(1, count):
        pl.semaphore_signal(barrier, 1, device_id={"elem": lax.rem(me + k, count)})

    def remote(src, dst, send, recv, device):
        return pltpu.make_async_remote_copy(
            src, dst, send, recv, device_id={"elem": device}, device_id_type=pl.DeviceIdType.MESH
        )

    row = lax.broadcasted_iota(jnp.int32, (rows, n), 0)
    lam = wave_square(lax.axis_index("mode") * mode_dev + row // 2, mode_total)

    def banded(v, ref):
        return mul_split(jnp.concatenate([v, lam * v], axis=1), ref[0], ref[1])

    def per_mode(v, ref, *at):
        vh, vl = split(v)
        both = jnp.concatenate([vh, vl], axis=0)
        sides = lax.broadcasted_iota(jnp.int32, both.shape, 0)
        sides = jnp.where(sides < rows, sides, sides - rows) // 2
        zero = jnp.zeros_like(both)
        total = None
        low = None
        for m in range(mode_dev):
            mine = jnp.where(sides == m, both, zero)
            term = bdot(mine, ref[(m,) + at + (0,)])
            term_low = bdot(mine[:rows], ref[(m,) + at + (1,)])
            total = term if total is None else total + term
            low = term_low if low is None else low + term_low
        return total[:rows] + (total[rows:] + low)

    def send_map(i, k, start):
        owner = half * core + i
        away = jnp.logical_and(owner != chip, chip > 0)
        if k < 2:
            away = jnp.logical_and(away, chip < chips - 1)

        @pl.when(away)
        def _():
            copy = remote(
                s.chip_maps.at[i, k],
                s.own_maps.at[chip, k],
                s.sem_cm_s.at[i, k],
                s.sem_cm_r.at[chip, k],
                2 * owner + core,
            )
            copy.start() if start else copy.wait_send()

    def share_copy(k, taken):
        block = s.both.at[core, pl.ds(half * jnp.where(taken == 0, other, core) + turn(k), 1)]
        return remote(block, block, s.sem_pm_s.at[taken, k], s.sem_pm_r.at[taken, k], partner)

    def pairing(k):
        share_copy(k, 0).wait()
        i = turn(k)
        one, two = ([split(s.both[c, half * core + i, k]) for k in range(3)] for c in range(2))
        s.chip_maps[i, 0] = times(one[0], two[0])
        s.chip_maps[i, 1] = times(two[1], one[1])
        s.chip_maps[i, 2] = s.both[0, half * core + i, 2] + times(split(times(one[0], two[2])), one[1])
        for k in (0, 2, 1):
            send_map(i, k, True)

        @pl.when(half * core + i == chip)
        def _():
            s.own_maps[chip] = s.chip_maps[i]

    fetch["band"].wait()
    first = line * mode_dev

    def part_step(k, carry):
        panel_copy(k, 0).wait()
        panel_copy(k, 1).wait()
        mode_maps(s, core, [half * other + turn(k), half * core + turn(k)], first, mode_total)

        @pl.when(k == 0)
        def _():
            pl.semaphore_wait(barrier, mode_axis - 1 + count - 1)

        share_copy(k, 0).start()
        share_copy(k, 1).start()

        @pl.when(k > 0)
        def _():
            pairing(k - 1)

        return carry

    lax.fori_loop(0, half, part_step, 0)

    fetch["rhs"].wait()
    fetch["table"].wait()
    rhs = split(s.rhs[...])
    spectrum = bdot_turned(s.table[0], rhs[0]) + (bdot_turned(s.table[1], rhs[0]) + bdot_turned(s.table[0], rhs[1]))
    s.spec_out[...] = spectrum.reshape(s.spec_out.shape)

    def spread_out(k, carry):
        to = lax.rem(line + k, mode_axis)
        pltpu.make_async_remote_copy(
            s.spec_out.at[to],
            s.spec_in.at[line],
            s.sem_sp.at[0],
            s.sem_sp.at[1],
            device_id={"mode": to},
            device_id_type=pl.DeviceIdType.MESH,
        ).start()
        return carry

    lax.fori_loop(1, mode_axis, spread_out, 0)
    s.spec_in[line] = s.spec_out[line]

    pairing(half - 1)
    for name in ("radial", "stiff", "mass"):
        fetch[name].wait()
    slab_matrices(s, number_ref)

    for k in range(half):
        share_copy(k, 1).wait()

    def last_step(at):
        last_maps(s, core, [at * half + i for i in range(half)], first, mode_total)

    last_step(0)

    others = s.spec_in.at[pl.ds(0, mode_axis - 1)]
    pltpu.make_async_remote_copy(
        others, others, s.sem_sp.at[0], s.sem_sp.at[1], device_id={"mode": line}, device_id_type=pl.DeviceIdType.MESH
    ).wait()
    width = s.spec_in.shape[2]
    modal = []
    for t in range(slabs * (inner + 1)):
        pieces = []
        at = t * n
        while at < (t + 1) * n:
            source = at // width
            stop = min((t + 1) * n, (source + 1) * width)
            pieces.append(s.spec_in[source, :, at - source * width : stop - source * width])
            at = stop
        modal.append(pieces[0] if len(pieces) == 1 else jnp.concatenate(pieces, axis=1))

    spectral = []
    inverses = []
    sums = []
    fields = []
    for j in range(slabs):
        base = j * (inner + 1)
        x = jnp.concatenate([modal[base + a] for a in range(inner)], axis=0)
        fields.append(mul_split(x, s.rs[j, 0], s.rs[j, 1]))
    for j in range(slabs):
        x = fields[j]
        values = []
        scales = []
        for b in range(inner):
            total = x[:rows] * axial_ref[j, 0, b]
            for a in range(1, inner):
                total = total + x[a * rows : (a + 1) * rows] * axial_ref[j, a, b]
            scale = 1.0 / (axial_eig_ref[j, b] + radial_eig_ref[j : j + 1, :] + lam)
            scales.append(scale)
            values.append(total * scale)
        spectral.append(values)
        inverses.append(scales)
        faces = [None, None]
        for a in range(inner):
            total = values[0] * axial_ref[j, a, 0]
            for b in range(1, inner):
                total = total + values[b] * axial_ref[j, a, b]
            for side in range(2):
                term = total * couple_ref[j, side, a]
                faces[side] = term if faces[side] is None else faces[side] + term
        sums.append(faces)
        if j == 0:
            s.push_send[...] = banded(faces[0], s.push.at[0, 0])

            @pl.when(me > 0)
            def _():
                remote(s.push_send, s.placed_in, s.sem_pl.at[0], s.sem_pl.at[1], me - 1).start()

    placed = [
        [None if j + side == 0 else banded(sums[j][side], s.push.at[j, side]) for side in range(2)]
        for j in range(slabs)
    ]

    loads = [modal[j * (inner + 1) + inner] - placed[j][1] for j in range(slabs)]
    for j in range(slabs - 1):
        loads[j] = loads[j] - placed[j + 1][0]
    local = [per_mode(loads[0], s.pts, 0)]
    for j in range(1, slabs):
        load = loads[j] - banded(local[j - 1], s.ets.at[j - 1])
        if j == slabs - 1:

            @pl.when(me == count - 1)
            def _():
                s.placed_in[...] = jnp.zeros_like(s.placed_in)

            @pl.when(me < count - 1)
            def _():
                remote(s.push_send, s.placed_in, s.sem_pl.at[0], s.sem_pl.at[1], me).wait_recv()

            load = load - s.placed_in[...]
        local.append(per_mode(load, s.pts, j))
    offset = per_mode(local[0], s.uts, 0)
    for j in range(1, slabs):
        offset = offset + per_mode(local[j], s.uts, j)
    s.vec_send[...] = jnp.zeros_like(s.vec_send)
    for m in range(mode_dev):
        s.vec_send[m, 0:2, :] = local[-1][2 * m : 2 * m + 2]
        s.vec_send[m, 2:4, :] = offset[2 * m : 2 * m + 2]
    swap = remote(s.vec_send, s.mate_vecs, s.sem_pv.at[0], s.sem_pv.at[1], partner)
    swap.start()
    low = lax.broadcasted_iota(jnp.int32, (8, n), 0) < 2

    @pl.when(core == 0)
    def _():
        for m in range(mode_dev):
            tile = s.vec_send[m]
            turned = mul(mul(tile, s.both[1, m, 2]), s.both[0, m, 1])
            s.chip_vecs[m] = jnp.where(low, mul(tile, s.both[1, m, 0]), tile + pltpu.roll(turned, 2, 0))

    @pl.when(core == 1)
    def _():
        for m in range(mode_dev):
            tile = s.vec_send[m]
            s.chip_vecs[m] = jnp.where(low, tile, mul(tile, s.both[0, m, 1]))

    is_owner = chip // half == core
    for m in range(mode_dev):
        to = 2 * m + m // half

        @pl.when(me != to)
        def _():
            remote(s.chip_vecs.at[m], s.own_vecs.at[me], s.sem_cv.at[0], s.sem_cv.at[1], to).start()

        @pl.when(me == to)
        def _():
            s.own_vecs[me] = s.chip_vecs[m]

    def tiles(ref, number, sems):
        block = ref.at[pl.ds(0, number)]
        return remote(block, block, sems.at[0], sems.at[1], me)

    last_step(1)

    local_values = [None] * slabs
    local_values[-1] = local[-1]
    for j in reversed(range(slabs - 1)):
        local_values[j] = local[j] - per_mode(banded(local_values[j + 1], s.es.at[j]), s.pts, j)
    swap.wait()

    @pl.when(core == 0)
    def _():
        for m in range(mode_dev):
            turned = s.mate_vecs[m] + pltpu.roll(mul(s.vec_send[m], s.both[1, m, 2]), 2, 0)
            s.fin[m] = pltpu.roll(turned, 6, 0)

    @pl.when(core == 1)
    def _():
        s.fin[...] = s.mate_vecs[...]

    within = jnp.concatenate([s.fin[m, 0:2, :] for m in range(mode_dev)], axis=0)
    for j in range(slabs):
        local_values[j] = local_values[j] + per_mode(within, s.extra, j)

    @pl.when(is_owner)
    def _():
        tiles(s.own_vecs, count - 1, s.sem_cv).wait_recv()

        def arrived(z, k):
            @pl.when(z != chip)
            def _():
                remote(
                    s.chip_maps.at[0, k], s.own_maps.at[z, k], s.sem_cm_s.at[0, k], s.sem_cm_r.at[z, k], me
                ).wait_recv()

        for z in range(1, chips - 1):
            arrived(z, 0)
        vecs = [s.own_vecs[2 * z] + s.own_vecs[2 * z + 1] for z in range(chips)]
        state = jnp.zeros((8, n), F32)
        before = []
        for z in range(chips):
            before.append(state)
            if z == 0:
                state = vecs[z]
            elif z < chips - 1:
                state = mul(state, s.own_maps[z, 0]) + vecs[z]
        for z in range(1, chips):
            arrived(z, 2)
            if z < chips - 1:
                arrived(z, 1)
        terms = [vecs[0]]
        for z in range(1, chips):
            terms.append(vecs[z] + pltpu.roll(mul(before[z], s.own_maps[z, 2]), 2, 0))
        state = jnp.zeros((8, n), F32)
        for z in reversed(range(chips)):
            back = jnp.where(low, before[z], state)
            s.back_send[2 * z] = back
            s.back_send[2 * z + 1] = back
            if z > 0:
                state = terms[z] if z == chips - 1 else mul(state, s.own_maps[z, 1]) + terms[z]

        def answer(k, carry):
            to = lax.rem(me + k, count)
            remote(s.back_send.at[to], s.back_vecs.at[chip], s.sem_bk.at[0], s.sem_bk.at[1], to).start()
            return carry

        lax.fori_loop(1, count, answer, 0, unroll=True)
        s.back_vecs[chip] = s.back_send[me]
        tiles(s.back_vecs, mode_dev - 1, s.sem_bk).wait_recv()

    @pl.when(jnp.logical_not(is_owner))
    def _():
        tiles(s.back_vecs, mode_dev, s.sem_bk).wait_recv()

    start = jnp.concatenate([s.back_vecs[m, 0:2, :] for m in range(mode_dev)], axis=0)
    end = jnp.concatenate([s.back_vecs[m, 2:4, :] for m in range(mode_dev)], axis=0)
    bounds = jnp.concatenate([start, end], axis=1)
    values = [None] * slabs
    for j in reversed(range(slabs)):
        values[j] = local_values[j] + per_mode(bounds, s.last, j)
        if j == slabs - 1:
            s.x_send[...] = values[j]

            @pl.when(me < count - 1)
            def _():
                remote(s.x_send, s.x_in, s.sem_x.at[0], s.sem_x.at[1], me + 1).start()

    for j in reversed(range(slabs)):
        if j == 0:
            for i in range(half):
                for k in range(3):
                    send_map(i, k, False)

            @pl.when(is_owner)
            def _():
                tiles(s.chip_vecs, mode_dev - 1, s.sem_cv).wait_send()

            @pl.when(jnp.logical_not(is_owner))
            def _():
                tiles(s.chip_vecs, mode_dev, s.sem_cv).wait_send()

            @pl.when(me == 0)
            def _():
                s.x_in[...] = jnp.zeros_like(s.x_in)

            @pl.when(me > 0)
            def _():
                remote(s.x_send, s.x_in, s.sem_x.at[0], s.sem_x.at[1], me).wait_recv()

            faces = [s.x_in[...], values[0]]
        else:
            faces = [values[j - 1], values[j]]
        lifted = [banded(faces[side], s.lift.at[j, side]) for side in range(2)]
        spread = [
            lifted[0] * couple_ref[j, 0, a] + lifted[1] * couple_ref[j, 1, a] for a in range(inner)
        ]
        left = []
        for b in range(inner):
            total = spread[0] * axial_ref[j, 0, b]
            for a in range(1, inner):
                total = total + spread[a] * axial_ref[j, a, b]
            left.append(spectral[j][b] - total * inverses[j][b])
        turned = []
        for a in range(inner):
            total = left[0] * axial_ref[j, a, 0]
            for b in range(1, inner):
                total = total + left[b] * axial_ref[j, a, b]
            turned.append(total)
        result = mul_split(jnp.concatenate(turned, axis=0), s.rts[j, 0], s.rts[j, 1])
        base = j * (inner + 1) * n
        for a in range(inner):
            out_ref[:, base + a * n : base + (a + 1) * n] = result[a * rows : (a + 1) * rows]
        out_ref[:, base + inner * n : base + (inner + 1) * n] = values[j]

    @pl.when(me > 0)
    def _():
        remote(s.push_send, s.placed_in, s.sem_pl.at[0], s.sem_pl.at[1], me - 1).wait_send()

    @pl.when(me < count - 1)
    def _():
        remote(s.x_send, s.x_in, s.sem_x.at[0], s.sem_x.at[1], me + 1).wait_send()

    @pl.when(is_owner)
    def _():
        tiles(s.back_send, count - 1, s.sem_bk).wait_send()


def fourier_table(planes):
    row = np.arange(planes)[:, None]
    angles = (row // 2 * np.arange(planes)[None, :] % planes) * (2.0 * math.pi / planes)
    return (np.where(row % 2 == 0, np.cos(angles), -np.sin(angles)) / math.sqrt(planes)).astype(np.float32)


VMEM = pl.BlockSpec(memory_space=pltpu.VMEM)
SMEM = pl.BlockSpec(memory_space=pltpu.SMEM)
HBM = pl.BlockSpec(memory_space=pltpu.HBM)
LOADED = ("panel", "band", "rhs", "table", "radial", "stiff", "mass")


def body(
    rhs_phys,
    radial_basis,
    axial_basis,
    radial_eig,
    axial_eig,
    face_stiff,
    face_mass,
    axial_coupling,
    face_numbering,
    band_panels,
    inverse_panels,
):
    planes = rhs_phys.shape[0]
    mode_dev, slabs, n = inverse_panels.shape[:3]
    inner = axial_basis.shape[1]
    mode_axis = lax.axis_size("mode")
    chips = lax.axis_size("elem") // 2
    mode_total = mode_dev * mode_axis
    rows = 2 * mode_dev
    half = mode_dev // 2
    parts = half
    count = 2 * chips
    width = rhs_phys.shape[1]

    table = fourier_table(planes)
    table_high = table.astype(ml_dtypes.bfloat16)
    table = np.stack([table_high, (table - table_high.astype(np.float32)).astype(ml_dtypes.bfloat16)])
    loaded = (inverse_panels, band_panels, rhs_phys.T, jnp.asarray(table), radial_basis, face_stiff, face_mass)

    def V(*shape, dtype=F32):
        return pltpu.VMEM(shape, dtype)

    def D(*shape):
        return pltpu.SemaphoreType.DMA(shape)

    scratch = {name: V(*array.shape, dtype=array.dtype) for name, array in zip(LOADED, loaded)}
    scratch.update(
        rs=V(slabs, 2, n, n, dtype=BF16),
        rts=V(slabs, 2, n, n, dtype=BF16),
        push=V(slabs, 2, 2, 2 * n, n, dtype=BF16),
        lift=V(slabs, 2, 2, 2 * n, n, dtype=BF16),
        es=V(slabs - 1, 2, 2 * n, n, dtype=BF16),
        ets=V(slabs - 1, 2, 2 * n, n, dtype=BF16),
        pts=V(mode_dev, slabs, 2, n, n, dtype=BF16),
        uts=V(mode_dev, slabs, 2, n, n, dtype=BF16),
        nts=V(mode_dev, slabs, 2, n, n, dtype=BF16),
        last=V(mode_dev, slabs, 2, 2 * n, n, dtype=BF16),
        extra=V(mode_dev, slabs, 2, n, n, dtype=BF16),
        spec_out=V(mode_axis, rows, width),
        spec_in=V(mode_axis, rows, width),
        placed_in=V(rows, n),
        x_in=V(rows, n),
        x_send=V(rows, n),
        push_send=V(rows, n),
        both=V(2, mode_dev, 3, n, n),
        chip_maps=V(half, 3, n, n),
        own_maps=V(chips, 3, n, n),
        vec_send=V(mode_dev, 8, n),
        mate_vecs=V(mode_dev, 8, n),
        chip_vecs=V(mode_dev, 8, n),
        own_vecs=V(count, 8, n),
        back_send=V(count, 8, n),
        back_vecs=V(mode_dev, 8, n),
        fin=V(mode_dev, 8, n),
        sem_in=D(len(LOADED) - 1),
        sem_pa=D(parts, 2),
        sem_sp=D(2),
        sem_pm_s=D(2, parts),
        sem_pm_r=D(2, parts),
        sem_cm_s=D(half, 3),
        sem_cm_r=D(chips, 3),
        sem_pl=D(2),
        sem_pv=D(2),
        sem_cv=D(2),
        sem_bk=D(2),
        sem_x=D(2),
    )
    names = [name + "_hbm" for name in LOADED] + ["out"] + list(scratch)
    return pl.pallas_call(
        functools.partial(solve_kernel, names, mode_axis, mode_dev, mode_total, chips),
        out_shape=jax.ShapeDtypeStruct((rows, slabs * (inner + 1) * n), F32),
        in_specs=[SMEM] * 3 + [VMEM] * 2 + [HBM] * len(LOADED),
        out_specs=VMEM,
        scratch_shapes=list(scratch.values()),
        compiler_params=pltpu.CompilerParams(
            collective_id=0, has_side_effects=True, vmem_limit_bytes=56 << 20
        ),
        name="pressure_solve",
    )(
        axial_basis,
        axial_coupling,
        axial_eig,
        radial_eig,
        face_numbering,
        *loaded,
    )


def solution(mesh):
    placed = (
        P(None, ("elem", "mode")),
        P("elem", None, None),
        P("elem", None, None),
        P("elem", None),
        P("elem", None),
        P("elem", None, None),
        P("elem", None, None),
        P("elem", None, None),
        P("elem", None, None),
        P(None, "elem", None, None),
        P("mode", "elem", None, None),
    )
    return jax.shard_map(
        body, mesh=mesh, in_specs=placed, out_specs=P("mode", "elem"), check_vma=False
    )
```

```python
import functools
import math
from types import SimpleNamespace

import jax
import jax.numpy as jnp
import ml_dtypes
import numpy as np
from jax import lax
from jax.experimental import pallas as pl
from jax.experimental.pallas import tpu as pltpu
from jax.sharding import PartitionSpec as P

F32 = jnp.float32
BF16 = jnp.bfloat16


def split(x):
    hi = x.astype(BF16)
    return hi, (x - hi.astype(F32)).astype(BF16)


def bdot(a, b):
    return jnp.dot(a, b, preferred_element_type=F32)


def bdot_turned(a, b):
    return lax.dot_general(a, b, (((1,), (1,)), ((), ())), preferred_element_type=F32)


def mul_split(v, hi, lo):
    vh, vl = split(v)
    rows = v.shape[0]
    if rows <= 16:
        both = bdot(jnp.concatenate([vh, vl], axis=0), hi)
        return both[:rows] + (both[rows:] + bdot(vh, lo))
    return bdot(vh, hi) + (bdot(vl, hi) + bdot(vh, lo))


def mul(a, b):
    return mul_split(a, *split(b))


def wave_square(index, mode_total):
    wave = index.astype(F32) / mode_total
    return 4.0 * wave * wave


def store_split(ref, at, x):
    hi, lo = split(x)
    ref[at + (0,)] = hi
    ref[at + (1,)] = lo


def slab_matrices(s, number_ref):
    slabs, n = s.radial.shape[0], s.radial.shape[1]
    turned = []
    for j in range(slabs):
        basis = s.radial[j]
        store_split(s.rs, (j,), basis)
        store_split(s.rts, (j,), basis.T)
        for face in (s.stiff, s.mass):
            turned.append(split(mul(face[j].T, basis)))
    for j in range(slabs):
        for side in range(2):
            numbers = number_ref[j, side : side + 1, :]
            hot = (lax.broadcasted_iota(jnp.int32, (n, n), 0) == numbers).astype(F32).astype(BF16)
            for part in range(2):
                th, tl = turned[2 * j + part]
                kt = bdot(hot, th) + bdot(hot, tl)
                for ref, x in ((s.lift, kt), (s.push, kt.T)):
                    hi, lo = split(x)
                    ref[j, side, 0, part * n : (part + 1) * n, :] = hi
                    ref[j, side, 1, part * n : (part + 1) * n, :] = lo
    for j in range(1, slabs):
        for part in range(2):
            band = s.band[part, j]
            for ref, x in ((s.es, band), (s.ets, band.T)):
                hi, lo = split(x)
                ref[j - 1, 0, part * n : (part + 1) * n, :] = hi
                ref[j - 1, 1, part * n : (part + 1) * n, :] = lo


def times(a, b):
    return bdot(a[0], b[0]) + (bdot(a[1], b[0]) + bdot(a[0], b[1]))


def mode_maps(s, core, modes, first, mode_total):
    slabs = s.panel.shape[1]
    count = len(modes)
    turned = [[s.band[p, j].T for p in range(2)] for j in range(slabs)]
    lams = [wave_square(first + m, mode_total) for m in modes]
    es = [[split(s.band[0, j] + lam * s.band[1, j]) for j in range(slabs)] for lam in lams]
    ets = [[split(turned[j][0] + lam * turned[j][1]) for j in range(slabs)] for lam in lams]
    pts = [[split(s.panel[m, j].T) for j in range(slabs)] for m in modes]
    for i, m in enumerate(modes):
        for j in range(slabs):
            s.pts[m, j, 0] = pts[i][j][0]
            s.pts[m, j, 1] = pts[i][j][1]
    ahead = [ets[i][0] for i in range(count)]
    back = [es[i][0] for i in range(count)]
    cross = [None] * count
    nears = [[] for _ in modes]
    for j in range(slabs):
        if j > 0:
            for i in range(count):
                ahead[i] = split(times(ahead[i], ets[i][j]))
                back[i] = split(times(es[i][j], back[i]))
        for i, m in enumerate(modes):
            s.uts[m, j, 0] = back[i][0]
            s.uts[m, j, 1] = back[i][1]
            full = -times(ahead[i], pts[i][j])
            ahead[i] = split(full)
            s.nts[m, j, 0] = ahead[i][0]
            s.nts[m, j, 1] = ahead[i][1]
            nears[i].append((ahead[i], back[i]))
            backed = -times(pts[i][j], back[i])
            back[i] = split(backed)
            if j == slabs - 1:
                s.both[core, m, 0] = full
                s.both[core, m, 1] = backed
    for j in range(slabs):
        for i in range(count):
            term = times(*nears[i][j])
            cross[i] = term if cross[i] is None else cross[i] + term
    for i, m in enumerate(modes):
        s.both[core, m, 2] = cross[i]


def last_maps(s, core, modes, first, mode_total):
    slabs, n = s.panel.shape[1], s.panel.shape[2]
    where = range(len(modes))
    lams = [wave_square(first + m, mode_total) for m in modes]
    bands = [[split(s.band[0, j] + lam * s.band[1, j]) for j in range(1, slabs)] for lam in lams]
    turns = [[times(bands[i][j], (s.pts[m, j, 0], s.pts[m, j, 1])) for j in range(slabs - 1)] for i, m in enumerate(modes)]
    turns = [[split(x) for x in row] for row in turns]
    near = [[None] * slabs for _ in modes]
    far = [[None] * slabs for _ in modes]
    for i, m in enumerate(modes):
        last = slabs - 1
        near[i][last] = (s.nts[m, last, 0], s.nts[m, last, 1])
        far[i][last] = (-s.pts[m, last, 0], -s.pts[m, last, 1])
    for j in reversed(range(slabs - 1)):
        for i, m in enumerate(modes):
            here = s.nts[m, j, 0].astype(F32) + s.nts[m, j, 1].astype(F32)
            near[i][j] = split(here - times(near[i][j + 1], turns[i][j]))
            far[i][j] = split(-times(far[i][j + 1], turns[i][j]))

    @pl.when(core == 0)
    def _():
        outer = [split(s.both[1, m, 1]) for m in modes]
        cross = [split(mul(s.both[0, m, 0], s.both[1, m, 2])) for m in modes]
        for j in range(slabs):
            for i, m in enumerate(modes):
                whole = near[i][j][0].astype(F32) + near[i][j][1].astype(F32)
                starts = split(whole + times(cross[i], far[i][j]))
                ends = split(times(outer[i], far[i][j]))
                for part in range(2):
                    s.last[m, j, part, 0:n] = starts[part]
                    s.last[m, j, part, n : 2 * n] = ends[part]
                    s.extra[m, j, part] = far[i][j][part]

    @pl.when(core == 1)
    def _():
        inner = [split(s.both[0, m, 0]) for m in modes]
        for j in range(slabs):
            for i, m in enumerate(modes):
                starts = split(times(inner[i], near[i][j]))
                for part in range(2):
                    s.last[m, j, part, 0:n] = starts[part]
                    s.last[m, j, part, n : 2 * n] = far[i][j][part]
                    s.extra[m, j, part] = near[i][j][part]


def solve_kernel(
    names,
    mode_axis,
    mode_dev,
    mode_total,
    chips,
    axial_ref,
    couple_ref,
    axial_eig_ref,
    radial_eig_ref,
    number_ref,
    *refs,
):
    s = SimpleNamespace(**dict(zip(names, refs)))
    out_ref = s.out
    slabs, n = s.rs.shape[0], s.rs.shape[-1]
    rows = 2 * mode_dev
    half = mode_dev // 2
    inner = axial_ref.shape[1]
    me = lax.axis_index("elem")
    count = 2 * chips
    core = lax.rem(me, 2)
    chip = me // 2
    other = 1 - core
    partner = 2 * chip + other

    parts = [[lax.rem(chip + k, half)] for k in range(half)]
    fetch = {}
    for at, name in enumerate(LOADED[1:]):
        copy = pltpu.make_async_copy(getattr(s, name + "_hbm"), getattr(s, name), s.sem_in.at[at])
        copy.start()
        fetch[name] = copy
        if at == 0:
            panels = []
            for k, part in enumerate(parts):
                for j, whose in enumerate((other, core)):
                    block = pl.ds(half * whose + part[0], len(part))
                    copy = pltpu.make_async_copy(s.panel_hbm.at[block], s.panel.at[block], s.sem_pa.at[k, j])
                    copy.start()
                    panels.append(copy)

    barrier = pltpu.get_barrier_semaphore()
    line = lax.axis_index("mode")
    for k in range(1, mode_axis):
        pl.semaphore_signal(barrier, 1, device_id={"mode": lax.rem(line + k, mode_axis)})
    for k in range(1, count):
        pl.semaphore_signal(barrier, 1, device_id={"elem": lax.rem(me + k, count)})

    def remote(src, dst, send, recv, device):
        return pltpu.make_async_remote_copy(
            src, dst, send, recv, device_id={"elem": device}, device_id_type=pl.DeviceIdType.MESH
        )

    row = lax.broadcasted_iota(jnp.int32, (rows, n), 0)
    lam = wave_square(lax.axis_index("mode") * mode_dev + row // 2, mode_total)

    def banded(v, ref):
        return mul_split(jnp.concatenate([v, lam * v], axis=1), ref[0], ref[1])

    def per_mode(v, ref, *at):
        vh, vl = split(v)
        both = jnp.concatenate([vh, vl], axis=0)
        sides = lax.broadcasted_iota(jnp.int32, both.shape, 0)
        sides = jnp.where(sides < rows, sides, sides - rows) // 2
        zero = jnp.zeros_like(both)
        total = None
        low = None
        for m in range(mode_dev):
            mine = jnp.where(sides == m, both, zero)
            term = bdot(mine, ref[(m,) + at + (0,)])
            term_low = bdot(mine[:rows], ref[(m,) + at + (1,)])
            total = term if total is None else total + term
            low = term_low if low is None else low + term_low
        return total[:rows] + (total[rows:] + low)

    def send_map(i, k, start):
        owner = half * core + i
        away = jnp.logical_and(owner != chip, chip > 0)
        if k < 2:
            away = jnp.logical_and(away, chip < chips - 1)

        @pl.when(away)
        def _():
            copy = remote(
                s.chip_maps.at[i, k],
                s.own_maps.at[chip, k],
                s.sem_cm_s.at[i, k],
                s.sem_cm_r.at[chip, k],
                2 * owner + core,
            )
            copy.start() if start else copy.wait_send()

    def pairing(part, share):
        share.wait()
        pair = [[[split(s.both[c, half * core + i, k]) for k in range(3)] for c in range(2)] for i in part]
        ahead = [times(one[0][0], one[1][0]) for one in pair]
        back = [times(one[1][1], one[0][1]) for one in pair]
        cross = [split(times(one[0][0], one[1][2])) for one in pair]
        cross = [times(x, one[0][1]) for x, one in zip(cross, pair)]
        for at, i in enumerate(part):
            s.chip_maps[i, 0] = ahead[at]
            s.chip_maps[i, 1] = back[at]
            s.chip_maps[i, 2] = s.both[0, half * core + i, 2] + cross[at]
        for i in part:
            for k in (0, 2, 1):
                send_map(i, k, True)

            @pl.when(half * core + i == chip)
            def _():
                s.own_maps[chip] = s.chip_maps[i]

    fetch["band"].wait()
    first = line * mode_dev
    shares = [[], []]
    for at, part in enumerate(parts):
        modes = [half * other + i for i in part] + [half * core + i for i in part]
        for copy in panels[2 * at : 2 * at + 2]:
            copy.wait()
        mode_maps(s, core, modes, first, mode_total)
        if at == 0:
            pl.semaphore_wait(barrier, mode_axis - 1 + count - 1)
        for whose, taken in ((other, 0), (core, 1)):
            block = s.both.at[core, pl.ds(half * whose + part[0], len(part))]
            share = remote(block, block, s.sem_pm_s.at[taken, at], s.sem_pm_r.at[taken, at], partner)
            share.start()
            shares[taken].append(share)
        if at > 0:
            pairing(parts[at - 1], shares[0][at - 1])

    fetch["rhs"].wait()
    fetch["table"].wait()
    rhs = split(s.rhs[...])
    spectrum = bdot_turned(s.table[0], rhs[0]) + (bdot_turned(s.table[1], rhs[0]) + bdot_turned(s.table[0], rhs[1]))
    s.spec_out[...] = spectrum.reshape(s.spec_out.shape)

    def spread_out(k, carry):
        to = lax.rem(line + k, mode_axis)
        pltpu.make_async_remote_copy(
            s.spec_out.at[to],
            s.spec_in.at[line],
            s.sem_sp.at[0],
            s.sem_sp.at[1],
            device_id={"mode": to},
            device_id_type=pl.DeviceIdType.MESH,
        ).start()
        return carry

    lax.fori_loop(1, mode_axis, spread_out, 0)
    s.spec_in[line] = s.spec_out[line]

    pairing(parts[-1], shares[0][-1])
    for name in ("radial", "stiff", "mass"):
        fetch[name].wait()
    slab_matrices(s, number_ref)

    for share in shares[1]:
        share.wait()
    for at in range(0, mode_dev, half):
        last_maps(s, core, range(at, at + half), first, mode_total)

    others = s.spec_in.at[pl.ds(0, mode_axis - 1)]
    pltpu.make_async_remote_copy(
        others, others, s.sem_sp.at[0], s.sem_sp.at[1], device_id={"mode": line}, device_id_type=pl.DeviceIdType.MESH
    ).wait()
    width = s.spec_in.shape[2]
    modal = []
    for t in range(slabs * (inner + 1)):
        pieces = []
        at = t * n
        while at < (t + 1) * n:
            source = at // width
            stop = min((t + 1) * n, (source + 1) * width)
            pieces.append(s.spec_in[source, :, at - source * width : stop - source * width])
            at = stop
        modal.append(pieces[0] if len(pieces) == 1 else jnp.concatenate(pieces, axis=1))

    spectral = []
    inverses = []
    sums = []
    fields = []
    for j in range(slabs):
        base = j * (inner + 1)
        x = jnp.concatenate([modal[base + a] for a in range(inner)], axis=0)
        fields.append(mul_split(x, s.rs[j, 0], s.rs[j, 1]))
    for j in range(slabs):
        x = fields[j]
        values = []
        scales = []
        for b in range(inner):
            total = x[:rows] * axial_ref[j, 0, b]
            for a in range(1, inner):
                total = total + x[a * rows : (a + 1) * rows] * axial_ref[j, a, b]
            scale = 1.0 / (axial_eig_ref[j, b] + radial_eig_ref[j : j + 1, :] + lam)
            scales.append(scale)
            values.append(total * scale)
        spectral.append(values)
        inverses.append(scales)
        faces = [None, None]
        for a in range(inner):
            total = values[0] * axial_ref[j, a, 0]
            for b in range(1, inner):
                total = total + values[b] * axial_ref[j, a, b]
            for side in range(2):
                term = total * couple_ref[j, side, a]
                faces[side] = term if faces[side] is None else faces[side] + term
        sums.append(faces)
        if j == 0:
            s.push_send[...] = banded(faces[0], s.push.at[0, 0])

            @pl.when(me > 0)
            def _():
                remote(s.push_send, s.placed_in, s.sem_pl.at[0], s.sem_pl.at[1], me - 1).start()

    placed = [
        [None if j + side == 0 else banded(sums[j][side], s.push.at[j, side]) for side in range(2)]
        for j in range(slabs)
    ]

    loads = [modal[j * (inner + 1) + inner] - placed[j][1] for j in range(slabs)]
    for j in range(slabs - 1):
        loads[j] = loads[j] - placed[j + 1][0]
    local = [per_mode(loads[0], s.pts, 0)]
    for j in range(1, slabs):
        load = loads[j] - banded(local[j - 1], s.ets.at[j - 1])
        if j == slabs - 1:

            @pl.when(me == count - 1)
            def _():
                s.placed_in[...] = jnp.zeros_like(s.placed_in)

            @pl.when(me < count - 1)
            def _():
                remote(s.push_send, s.placed_in, s.sem_pl.at[0], s.sem_pl.at[1], me).wait_recv()

            load = load - s.placed_in[...]
        local.append(per_mode(load, s.pts, j))
    offset = per_mode(local[0], s.uts, 0)
    for j in range(1, slabs):
        offset = offset + per_mode(local[j], s.uts, j)
    s.vec_send[...] = jnp.zeros_like(s.vec_send)
    for m in range(mode_dev):
        s.vec_send[m, 0:2, :] = local[-1][2 * m : 2 * m + 2]
        s.vec_send[m, 2:4, :] = offset[2 * m : 2 * m + 2]
    swap = remote(s.vec_send, s.mate_vecs, s.sem_pv.at[0], s.sem_pv.at[1], partner)
    swap.start()
    low = lax.broadcasted_iota(jnp.int32, (8, n), 0) < 2

    @pl.when(core == 0)
    def _():
        for m in range(mode_dev):
            tile = s.vec_send[m]
            turned = mul(mul(tile, s.both[1, m, 2]), s.both[0, m, 1])
            s.chip_vecs[m] = jnp.where(low, mul(tile, s.both[1, m, 0]), tile + pltpu.roll(turned, 2, 0))

    @pl.when(core == 1)
    def _():
        for m in range(mode_dev):
            tile = s.vec_send[m]
            s.chip_vecs[m] = jnp.where(low, tile, mul(tile, s.both[0, m, 1]))

    is_owner = chip // half == core
    for m in range(mode_dev):
        to = 2 * m + m // half

        @pl.when(me != to)
        def _():
            remote(s.chip_vecs.at[m], s.own_vecs.at[me], s.sem_cv.at[0], s.sem_cv.at[1], to).start()

        @pl.when(me == to)
        def _():
            s.own_vecs[me] = s.chip_vecs[m]

    def tiles(ref, number, sems):
        block = ref.at[pl.ds(0, number)]
        return remote(block, block, sems.at[0], sems.at[1], me)

    local_values = [None] * slabs
    local_values[-1] = local[-1]
    for j in reversed(range(slabs - 1)):
        local_values[j] = local[j] - per_mode(banded(local_values[j + 1], s.es.at[j]), s.pts, j)
    swap.wait()

    @pl.when(core == 0)
    def _():
        for m in range(mode_dev):
            turned = s.mate_vecs[m] + pltpu.roll(mul(s.vec_send[m], s.both[1, m, 2]), 2, 0)
            s.fin[m] = pltpu.roll(turned, 6, 0)

    @pl.when(core == 1)
    def _():
        s.fin[...] = s.mate_vecs[...]

    within = jnp.concatenate([s.fin[m, 0:2, :] for m in range(mode_dev)], axis=0)
    for j in range(slabs):
        local_values[j] = local_values[j] + per_mode(within, s.extra, j)

    @pl.when(is_owner)
    def _():
        tiles(s.own_vecs, count - 1, s.sem_cv).wait_recv()

        def arrived(z, k):
            @pl.when(z != chip)
            def _():
                remote(
                    s.chip_maps.at[0, k], s.own_maps.at[z, k], s.sem_cm_s.at[0, k], s.sem_cm_r.at[z, k], me
                ).wait_recv()

        for z in range(1, chips - 1):
            arrived(z, 0)
        vecs = [s.own_vecs[2 * z] + s.own_vecs[2 * z + 1] for z in range(chips)]
        state = jnp.zeros((8, n), F32)
        before = []
        for z in range(chips):
            before.append(state)
            if z == 0:
                state = vecs[z]
            elif z < chips - 1:
                state = mul(state, s.own_maps[z, 0]) + vecs[z]
        for z in range(1, chips):
            arrived(z, 2)
            if z < chips - 1:
                arrived(z, 1)
        terms = [vecs[0]]
        for z in range(1, chips):
            terms.append(vecs[z] + pltpu.roll(mul(before[z], s.own_maps[z, 2]), 2, 0))
        state = jnp.zeros((8, n), F32)
        for z in reversed(range(chips)):
            back = jnp.where(low, before[z], state)
            s.back_send[2 * z] = back
            s.back_send[2 * z + 1] = back
            if z > 0:
                state = terms[z] if z == chips - 1 else mul(state, s.own_maps[z, 1]) + terms[z]

        def answer(k, carry):
            to = lax.rem(me + k, count)
            remote(s.back_send.at[to], s.back_vecs.at[chip], s.sem_bk.at[0], s.sem_bk.at[1], to).start()
            return carry

        lax.fori_loop(1, count, answer, 0, unroll=True)
        s.back_vecs[chip] = s.back_send[me]
        tiles(s.back_vecs, mode_dev - 1, s.sem_bk).wait_recv()

    @pl.when(jnp.logical_not(is_owner))
    def _():
        tiles(s.back_vecs, mode_dev, s.sem_bk).wait_recv()

    start = jnp.concatenate([s.back_vecs[m, 0:2, :] for m in range(mode_dev)], axis=0)
    end = jnp.concatenate([s.back_vecs[m, 2:4, :] for m in range(mode_dev)], axis=0)
    bounds = jnp.concatenate([start, end], axis=1)
    values = [None] * slabs
    for j in reversed(range(slabs)):
        values[j] = local_values[j] + per_mode(bounds, s.last, j)
        if j == slabs - 1:
            s.x_send[...] = values[j]

            @pl.when(me < count - 1)
            def _():
                remote(s.x_send, s.x_in, s.sem_x.at[0], s.sem_x.at[1], me + 1).start()

    for j in reversed(range(slabs)):
        right = banded(values[j], s.lift.at[j, 1])
        if j == 0:
            for i in range(half):
                for k in range(3):
                    send_map(i, k, False)

            @pl.when(is_owner)
            def _():
                tiles(s.chip_vecs, mode_dev - 1, s.sem_cv).wait_send()

            @pl.when(jnp.logical_not(is_owner))
            def _():
                tiles(s.chip_vecs, mode_dev, s.sem_cv).wait_send()

            @pl.when(me == 0)
            def _():
                s.x_in[...] = jnp.zeros_like(s.x_in)

            @pl.when(me > 0)
            def _():
                remote(s.x_send, s.x_in, s.sem_x.at[0], s.sem_x.at[1], me).wait_recv()

            left_face = s.x_in[...]
        else:
            left_face = values[j - 1]
        lifted = [banded(left_face, s.lift.at[j, 0]), right]
        spread = [
            lifted[0] * couple_ref[j, 0, a] + lifted[1] * couple_ref[j, 1, a] for a in range(inner)
        ]
        left = []
        for b in range(inner):
            total = spread[0] * axial_ref[j, 0, b]
            for a in range(1, inner):
                total = total + spread[a] * axial_ref[j, a, b]
            left.append(spectral[j][b] - total * inverses[j][b])
        turned = []
        for a in range(inner):
            total = left[0] * axial_ref[j, a, 0]
            for b in range(1, inner):
                total = total + left[b] * axial_ref[j, a, b]
            turned.append(total)
        result = mul_split(jnp.concatenate(turned, axis=0), s.rts[j, 0], s.rts[j, 1])
        base = j * (inner + 1) * n
        for a in range(inner):
            out_ref[:, base + a * n : base + (a + 1) * n] = result[a * rows : (a + 1) * rows]
        out_ref[:, base + inner * n : base + (inner + 1) * n] = values[j]

    @pl.when(me > 0)
    def _():
        remote(s.push_send, s.placed_in, s.sem_pl.at[0], s.sem_pl.at[1], me - 1).wait_send()

    @pl.when(me < count - 1)
    def _():
        remote(s.x_send, s.x_in, s.sem_x.at[0], s.sem_x.at[1], me + 1).wait_send()

    @pl.when(is_owner)
    def _():
        tiles(s.back_send, count - 1, s.sem_bk).wait_send()


def fourier_table(planes):
    row = np.arange(planes)[:, None]
    angles = (row // 2 * np.arange(planes)[None, :] % planes) * (2.0 * math.pi / planes)
    return (np.where(row % 2 == 0, np.cos(angles), -np.sin(angles)) / math.sqrt(planes)).astype(np.float32)


VMEM = pl.BlockSpec(memory_space=pltpu.VMEM)
SMEM = pl.BlockSpec(memory_space=pltpu.SMEM)
HBM = pl.BlockSpec(memory_space=pltpu.HBM)
LOADED = ("panel", "band", "rhs", "table", "radial", "stiff", "mass")


def body(
    rhs_phys,
    radial_basis,
    axial_basis,
    radial_eig,
    axial_eig,
    face_stiff,
    face_mass,
    axial_coupling,
    face_numbering,
    band_panels,
    inverse_panels,
):
    planes = rhs_phys.shape[0]
    mode_dev, slabs, n = inverse_panels.shape[:3]
    inner = axial_basis.shape[1]
    mode_axis = lax.axis_size("mode")
    chips = lax.axis_size("elem") // 2
    mode_total = mode_dev * mode_axis
    rows = 2 * mode_dev
    half = mode_dev // 2
    parts = half
    count = 2 * chips
    width = rhs_phys.shape[1]

    table = fourier_table(planes)
    table_high = table.astype(ml_dtypes.bfloat16)
    table = np.stack([table_high, (table - table_high.astype(np.float32)).astype(ml_dtypes.bfloat16)])
    loaded = (inverse_panels, band_panels, rhs_phys.T, jnp.asarray(table), radial_basis, face_stiff, face_mass)

    def V(*shape, dtype=F32):
        return pltpu.VMEM(shape, dtype)

    def D(*shape):
        return pltpu.SemaphoreType.DMA(shape)

    scratch = {name: V(*array.shape, dtype=array.dtype) for name, array in zip(LOADED, loaded)}
    scratch.update(
        rs=V(slabs, 2, n, n, dtype=BF16),
        rts=V(slabs, 2, n, n, dtype=BF16),
        push=V(slabs, 2, 2, 2 * n, n, dtype=BF16),
        lift=V(slabs, 2, 2, 2 * n, n, dtype=BF16),
        es=V(slabs - 1, 2, 2 * n, n, dtype=BF16),
        ets=V(slabs - 1, 2, 2 * n, n, dtype=BF16),
        pts=V(mode_dev, slabs, 2, n, n, dtype=BF16),
        uts=V(mode_dev, slabs, 2, n, n, dtype=BF16),
        nts=V(mode_dev, slabs, 2, n, n, dtype=BF16),
        last=V(mode_dev, slabs, 2, 2 * n, n, dtype=BF16),
        extra=V(mode_dev, slabs, 2, n, n, dtype=BF16),
        spec_out=V(mode_axis, rows, width),
        spec_in=V(mode_axis, rows, width),
        placed_in=V(rows, n),
        x_in=V(rows, n),
        x_send=V(rows, n),
        push_send=V(rows, n),
        both=V(2, mode_dev, 3, n, n),
        chip_maps=V(half, 3, n, n),
        own_maps=V(chips, 3, n, n),
        vec_send=V(mode_dev, 8, n),
        mate_vecs=V(mode_dev, 8, n),
        chip_vecs=V(mode_dev, 8, n),
        own_vecs=V(count, 8, n),
        back_send=V(count, 8, n),
        back_vecs=V(mode_dev, 8, n),
        fin=V(mode_dev, 8, n),
        sem_in=D(len(LOADED) - 1),
        sem_pa=D(parts, 2),
        sem_sp=D(2),
        sem_pm_s=D(2, parts),
        sem_pm_r=D(2, parts),
        sem_cm_s=D(half, 3),
        sem_cm_r=D(chips, 3),
        sem_pl=D(2),
        sem_pv=D(2),
        sem_cv=D(2),
        sem_bk=D(2),
        sem_x=D(2),
    )
    names = [name + "_hbm" for name in LOADED] + ["out"] + list(scratch)
    return pl.pallas_call(
        functools.partial(solve_kernel, names, mode_axis, mode_dev, mode_total, chips),
        out_shape=jax.ShapeDtypeStruct((rows, slabs * (inner + 1) * n), F32),
        in_specs=[SMEM] * 3 + [VMEM] * 2 + [HBM] * len(LOADED),
        out_specs=VMEM,
        scratch_shapes=list(scratch.values()),
        compiler_params=pltpu.CompilerParams(
            collective_id=0, has_side_effects=True, vmem_limit_bytes=56 << 20
        ),
        name="pressure_solve",
    )(
        axial_basis,
        axial_coupling,
        axial_eig,
        radial_eig,
        face_numbering,
        *loaded,
    )


def solution(mesh):
    placed = (
        P(None, ("elem", "mode")),
        P("elem", None, None),
        P("elem", None, None),
        P("elem", None),
        P("elem", None),
        P("elem", None, None),
        P("elem", None, None),
        P("elem", None, None),
        P("elem", None, None),
        P(None, "elem", None, None),
        P("mode", "elem", None, None),
    )
    return jax.shard_map(
        body, mesh=mesh, in_specs=placed, out_specs=P("mode", "elem"), check_vma=False
    )
```
